1024 devices in a mesh: wide: 64 (over y, x, core), narrow: 16 (over z).
Axes of the slice: x: 4, y: 8, z: 16, core: 2. Of those that a mesh axis runs over, the one named last changes fastest.
Arguments:
- gcm_state: float32 [8192, 144], P('wide'), may hold values from -6 to 6
- crm_state: bfloat16 [2, 60, 256, 8192], P(None, None, 'narrow', 'wide'), may hold values from -6 to 6
- courant: float32 [60, 8192], P(None, 'wide'), may hold values from 0.1 to 0.6
- cloud_mask: int32 [60, 8192], P(None, 'wide'), may hold values 0 or 1
- level_down: float32 [60, 72], replicated, may hold values from -0.75 to 0.75
- level_up: float32 [72, 60], replicated, may hold values from -0.75 to 0.75
- column_map: int32 [8192], replicated, may hold values from 0 to 8191, as said below
Outputs:
- gcm_tendency: bfloat16 [8192, 144], P('wide')
- crm_new: bfloat16 [2, 60, 256, 8192], P(None, None, 'narrow', 'wide')
The draws below stay inside these ranges and needn't reach their ends.
Inputs may be any that keep to these rules, and one draw needn't show every extreme that they name: column_map is a bijection onto 0 to 8191; the columns of one index of wide go to at most 4 slots of any one owner, and to exactly 4 slots of half of the owners.
All inputs are finite; a program needn't handle non-finite values. No bound on the sum of `cloud_mask` on one device may be relied on, other than what follows from the above.
Results may differ from the reference program's by a relative error of at most 0.0048.
Values may be sent and summed in bfloat16 or wider, within the bound.
No kernel may reach another device: no remote copies, remote signals or barrier semaphores. Data moves between devices by JAX's collectives and lax.ppermute only.
A program may use at most 32 MiB of HBM per device.

```python
import jax
import jax.numpy as jnp
from jax import lax

LEV = 72
CLEV = 60
CX = 256
SUB = 4
COLS_DEV = 128
NCOL = 8192
CAP = 4
N_WIDE = 64


def draw_column_map(key, part):
    rounds = N_WIDE // 2
    key_offsets = jax.random.fold_in(key, 11)
    key_places = jax.random.fold_in(key, 12)
    key_slots = jax.random.fold_in(key, 13)
    shuffled = jax.random.permutation(key_offsets, N_WIDE).astype(jnp.int32)
    rank_of = jnp.argsort(shuffled).astype(jnp.int32)
    values_all = jnp.arange(N_WIDE, dtype=jnp.int32)
    score = jnp.where(values_all == 1, -3, jnp.where(values_all == N_WIDE // 2, -2, jnp.where(values_all == N_WIDE - 1, -1, rank_of)))
    offsets = jnp.argsort(score)[:rounds].astype(jnp.int32)
    places = jax.vmap(lambda sub_key: jax.random.permutation(sub_key, COLS_DEV))(jax.random.split(key_places, N_WIDE)).astype(jnp.int32)
    slot_orders = jax.vmap(lambda sub_key: jax.random.permutation(sub_key, COLS_DEV))(jax.random.split(key_slots, N_WIDE)).astype(jnp.int32)
    source = jnp.arange(N_WIDE, dtype=jnp.int32)[:, None, None]
    round_index = jnp.arange(rounds, dtype=jnp.int32)[None, :, None]
    within = jnp.arange(CAP, dtype=jnp.int32)[None, None, :]
    owner = (source + offsets[round_index]) % N_WIDE
    local_index = round_index * CAP + within
    owner_full = jnp.broadcast_to(owner, (N_WIDE, rounds, CAP))
    local_full = jnp.broadcast_to(local_index, (N_WIDE, rounds, CAP))
    source_full = jnp.broadcast_to(source, (N_WIDE, rounds, CAP))
    slot_value = slot_orders[owner_full, local_full]
    place_value = places[source_full, local_full]
    target = owner_full * COLS_DEV + slot_value
    where_to = source_full * COLS_DEV + place_value
    return jnp.zeros((N_WIDE * COLS_DEV,), jnp.int32).at[where_to.reshape(-1)].set(target.reshape(-1))


def with_ends(values, own_key, smallest, largest):
    longest = values.shape.index(max(values.shape))
    spots = []
    for shift in (0, 1):
        where = [jax.random.randint(jax.random.fold_in(own_key, axis), (), 0, length) for axis, length in enumerate(values.shape)]
        where[longest] = (where[longest] + shift) % values.shape[longest]
        spots.append(tuple(where))
    return values.at[spots[0]].set(smallest).at[spots[1]].set(largest)


def block_levels(rng, dims, cuts, least, high):
    gain = 1.0
    for position, blocks in cuts:
        heights = jax.random.uniform(jax.random.fold_in(jax.random.fold_in(rng, 6), position), (blocks,), jnp.float32, least / len(cuts), high / len(cuts))
        gain = gain * jnp.repeat(jnp.exp(heights), dims[position] // blocks).reshape((-1,) + (1,) * (len(dims) - 1 - position))
    return gain


def bell_draw(own_key, extent, deviation, limit, cuts=(), held_as=jnp.bfloat16):
    values = deviation * jax.random.normal(own_key, extent, jnp.float32)
    if cuts:
        values = values * block_levels(own_key, extent, cuts, -0.22, 0.18)
    return jnp.clip(values, -limit, limit).astype(held_as)


def setup_inputs(seed: int = 0) -> dict:
    key_list = jax.random.split(jax.random.key(seed), 8)
    return {
        "gcm_state": bell_draw(key_list[0], (NCOL, 2 * LEV), 1.0, 6.0, ((0, 64),), jnp.float32),
        "crm_state": bell_draw(key_list[1], (2, CLEV, CX, NCOL), 1.0, 6.0, ((2, 16), (3, 64))),
        "courant": jnp.clip(0.1 + 0.5 * jax.random.uniform(key_list[2], (CLEV, NCOL), jnp.float32) ** block_levels(key_list[2], (CLEV, NCOL), ((1, 64),), -0.2, 0.2), 0.1, 0.6),
        "cloud_mask": with_ends((jax.random.randint(key_list[3], (CLEV, NCOL), 0, 2) < 1).astype(jnp.int32), jax.random.fold_in(key_list[3], 1), 0, 1),
        "level_down": bell_draw(key_list[4], (CLEV, LEV), LEV ** -0.5, 0.75, (), jnp.float32),
        "level_up": bell_draw(key_list[5], (LEV, CLEV), CLEV ** -0.5, 0.75, (), jnp.float32),
        "column_map": draw_column_map(jax.random.fold_in(key_list[7], 71), 0),
    }


def horizontal(padded, courant_now):
    left_cells = padded[:, :, :-2]
    middle = padded[:, :, 1:-1]
    right_cells = padded[:, :, 2:]
    return middle + courant_now[None, :, None, :] * (left_cells - middle) + 0.15 * (right_cells - 2.0 * middle + left_cells)


def column_physics(fields, forcing, cloudy):
    above_cells = jnp.concatenate([fields[:, 1:], fields[:, -1:]], axis=1)
    below_cells = jnp.concatenate([fields[:, :1], fields[:, :-1]], axis=1)
    fields = fields + 0.1 * (above_cells - 2.0 * fields + below_cells)
    fields = fields + 0.25 * forcing[:, :, None, :]
    moisture = fields[1]
    condensed = cloudy[:, None, :] * 0.3 * jnp.maximum(moisture, 0.0)
    return jnp.stack([fields[0] + 2.0 * condensed, moisture - condensed])


def crm_block(blocks):
    start_fields, forcing, courant_now, cloudy = blocks
    initial = start_fields.astype(jnp.float32)
    fields = initial
    for substep in range(SUB):
        padded = jnp.concatenate([fields[:, :, -1:], fields, fields[:, :, :1]], axis=2)
        fields = column_physics(horizontal(padded, courant_now), forcing, cloudy)
    return fields.astype(jnp.bfloat16), jnp.sum(fields - initial, axis=2)


def reference(gcm_state, crm_state, courant, cloud_mask, level_down, level_up, column_map):
    column_count = gcm_state.shape[0]
    sent_rows = lax.optimization_barrier(gcm_state.astype(jnp.bfloat16)).astype(jnp.float32)
    inverse = jnp.zeros((column_count,), jnp.int32).at[column_map].set(jnp.arange(column_count, dtype=jnp.int32))
    slot_rows = sent_rows[inverse].reshape(column_count, 2, LEV)
    forcing = jnp.einsum("sfm,lm->fls", slot_rows, level_down, precision=lax.Precision.HIGHEST)
    blocks_count = column_count // COLS_DEV

    def split_slots(values):
        return jnp.moveaxis(values.reshape(values.shape[:-1] + (blocks_count, COLS_DEV)), -2, 0)

    new_blocks, diff_blocks = lax.map(crm_block, (split_slots(crm_state), split_slots(forcing), split_slots(courant), split_slots(cloud_mask.astype(jnp.float32))))
    crm_new = jnp.moveaxis(new_blocks, 0, -2).reshape(crm_state.shape)
    diff_sums = jnp.moveaxis(diff_blocks, 0, -2).reshape(2, CLEV, column_count)
    tendency = jnp.einsum("fls,ml->sfm", diff_sums, level_up, precision=lax.Precision.HIGHEST) * (1.0 / (CX * SUB))
    gcm_tendency = tendency.reshape(column_count, 2 * LEV)[column_map].astype(jnp.bfloat16)
    return gcm_tendency, crm_new
```

```python
import functools

import jax
import jax.numpy as jnp
from jax import lax
from jax.experimental import pallas as pl
from jax.experimental.pallas import tpu as pltpu
from jax.sharding import PartitionSpec as P

CX = 256
SUB = 4
CAP = 4
ROWS = 6
LANES = 128
EXTRA = 16
HI = lax.Precision.HIGHEST
F32 = jnp.float32
BF16 = jnp.bfloat16


def iota(shape, dim):
    return lax.broadcasted_iota(jnp.int32, shape, dim)


def dot(a, b, dims):
    return lax.dot_general(a, b, (dims, ((), ())), preferred_element_type=F32)


def split3(x):
    a = x.astype(BF16)
    r = x - a.astype(F32)
    b = r.astype(BF16)
    c = (r - b.astype(F32)).astype(BF16)
    return a, b, c


def row_parts(n):
    row = iota((n, LANES), 0)
    peer = (row * 10923) >> 16
    return peer, row - peer * ROWS


def before_matrix():
    return (iota((LANES, LANES), 0) < iota((LANES, LANES), 1)).astype(BF16)


def pack_kernel(w_ref, map_ref, state_ref, wire_ref, owner_ref, rank_ref):
    peers = map_ref.shape[0]
    mine = map_ref[pl.ds(w_ref[0], 1), :] >> 7
    own = iota((peers, LANES), 0) == mine
    own_b = own.astype(BF16)
    count = dot(own_b, before_matrix(), ((1,), (0,)))
    rank = jnp.sum(jnp.where(own, count, 0.0), axis=0, keepdims=True).astype(jnp.int32)
    owner_ref[...] = own_b
    rank_ref[...] = jnp.broadcast_to(rank, rank_ref.shape)
    n = peers * ROWS
    peer, part = row_parts(n)
    to_peer = peer == mine
    main = (to_peer & (part == rank)).astype(BF16)
    tail = (to_peer & (part == CAP)).astype(BF16)
    state = state_ref[...].astype(BF16)
    levels = state.shape[0]
    extra = state[LANES:levels].astype(F32)
    spread = [jnp.where(rank == k, extra, 0.0) for k in range(CAP)]
    spread.append(jnp.zeros((LANES - CAP * EXTRA, LANES), F32))
    spread = jnp.concatenate(spread, axis=0).astype(BF16)
    wire = dot(main, state[:LANES], ((1,), (1,))) + dot(tail, spread, ((1,), (1,)))
    wire_ref[...] = wire.astype(BF16)


def route_kernel(w_ref, map_ref, slot_ref, take_ref, rank_ref):
    peers = map_ref.shape[0]
    targets = map_ref[...]
    here = (targets >> 7) == w_ref[0]
    local = (targets & (LANES - 1)).astype(F32) + 1.0
    count = dot(here.astype(BF16), before_matrix(), ((1,), (0,)))
    slots = []
    lane = iota((peers, LANES), 1).astype(F32) + 1.0
    for k in range(CAP):
        hit = here & (count == float(k))
        one = jnp.sum(jnp.where(hit, local, 0.0), axis=1, keepdims=True)
        slots.append((one == lane).astype(F32))
    rank = jnp.zeros((1, LANES), F32)
    anyslot = jnp.zeros((peers, LANES), F32)
    for k in range(CAP):
        rank = rank + float(k) * jnp.sum(slots[k], axis=0, keepdims=True)
        anyslot = anyslot + slots[k]
        slot_ref[:, k * LANES : (k + 1) * LANES] = slots[k].astype(BF16)
    rank_ref[...] = jnp.broadcast_to(rank, rank_ref.shape).astype(jnp.int32)
    n = peers * ROWS
    row = iota((n, peers), 0)
    peer = (row * 10923) >> 16
    part = row - peer * ROWS
    same = peer == iota((n, peers), 1)
    main = jnp.zeros((n, LANES), F32)
    for k in range(CAP):
        main = main + dot((same & (part == k)).astype(BF16), slots[k].astype(BF16), ((1,), (0,)))
    tail = dot((same & (part == CAP)).astype(BF16), anyslot.astype(BF16), ((1,), (0,)))
    take_ref[:, :LANES] = main.astype(BF16)
    take_ref[:, LANES:] = tail.astype(BF16)


def horizontal(x, a0, a1, keep=None):
    n = x.shape[0]
    left = pltpu.roll(x, 1, 0)
    right = pltpu.roll(x, n - 1, 0)
    if keep is not None:
        left, x, right = left[:keep], x[:keep], right[:keep]
    return a1 * left + a0 * x + 0.15 * right


def start_kernel(crm_ref, low_ref, high_ref, courant_ref, out_ref):
    levels = crm_ref.shape[1]

    def mixed(level):
        c = courant_ref[pl.ds(level, 1), :]
        a0, a1 = 0.7 - c, c + 0.15
        result = []
        for f in range(2):
            x = jnp.concatenate(
                [
                    crm_ref[f, level].astype(F32),
                    high_ref[f, level].astype(F32),
                    low_ref[f, level].astype(F32),
                ],
                axis=0,
            )
            result.append(horizontal(x, a0, a1))
        return tuple(result)

    def body(level, carry):
        below, here = carry
        above = mixed(jnp.minimum(level + 1, levels - 1))
        for f in range(2):
            out_ref[f, level] = 0.8 * here[f] + 0.1 * (above[f] + below[f])
        return here, above

    first = mixed(0)
    lax.fori_loop(0, levels, body, (first, first), unroll=4)


def main_kernel(
    wire_ref, take_ref, rank_ref, start_ref, crm_ref, courant_ref, mask_ref, down_ref,
    new_ref, diff_ref, force_ref, cloud_ref, field_ref,
):
    levels = crm_ref.shape[1]
    gcm = down_ref.shape[1]
    own = crm_ref.shape[2]
    got = dot(wire_ref[...], take_ref[...], ((0,), (0,)))
    tail = jnp.zeros((EXTRA, LANES), F32)
    rank = rank_ref[0:1, :]
    for k in range(CAP):
        tail = tail + jnp.where(rank == k, got[k * EXTRA : (k + 1) * EXTRA, LANES:], 0.0)
    rows = jnp.concatenate([got[:, :LANES], tail], axis=0)
    for f in range(2):
        force = lax.dot_general(
            down_ref[...], rows[f * gcm : (f + 1) * gcm], (((1,), (0,)), ((), ())),
            precision=HI, preferred_element_type=F32,
        )
        force_ref[f, :levels] = 0.25 * force
    cloud_ref[...] = mask_ref[...].astype(F32) * 0.3
    diff_ref[...] = jnp.zeros_like(diff_ref)

    def physics(pair, level):
        t = pair[0] + force_ref[0, pl.ds(level, 1), :]
        q = pair[1] + force_ref[1, pl.ds(level, 1), :]
        condensed = cloud_ref[pl.ds(level, 1), :] * jnp.maximum(q, 0.0)
        return t + 2.0 * condensed, q - condensed

    def substep(index):
        source = start_ref if index == 1 else field_ref
        last = index == SUB - 1
        keep = own if last else None

        def mixed(level):
            c = courant_ref[pl.ds(level, 1), :]
            a0, a1 = 0.7 - c, c + 0.15
            pair = (source[0, level], source[1, level])
            if index == 1:
                pair = physics(pair, level)
            return tuple(horizontal(x, a0, a1, keep) for x in pair)

        def body(level, carry):
            below, here = carry
            above = mixed(jnp.minimum(level + 1, levels - 1))
            pair = tuple(0.8 * here[f] + 0.1 * (above[f] + below[f]) for f in range(2))
            pair = physics(pair, level)
            for f in range(2):
                if last:
                    new_ref[f, level] = pair[f].astype(BF16)
                    change = pair[f] - crm_ref[f, level].astype(F32)
                    diff_ref[f, pl.ds(level, 1), :] = jnp.sum(change, axis=0, keepdims=True)
                else:
                    field_ref[f, level] = pair[f]
            return here, above

        first = mixed(0)
        lax.fori_loop(0, levels, body, (first, first), unroll=4)

    for index in range(1, SUB):
        substep(index)


def turn_kernel(part_ref, slot_ref, wire_ref):
    total = jnp.sum(part_ref[...], axis=0)
    peers = wire_ref.shape[0]
    rows = total.shape[0]
    wire = jnp.zeros((peers, LANES), F32)
    for piece in split3(total):
        for k in range(CAP):
            padded = []
            if k:
                padded.append(jnp.zeros((k * rows, LANES), F32))
            padded.append(piece.astype(F32))
            padded.append(jnp.zeros((LANES - (k + 1) * rows, LANES), F32))
            block = jnp.concatenate(padded, axis=0).astype(BF16)
            wire = wire + dot(slot_ref[:, k * LANES : (k + 1) * LANES], block, ((1,), (1,)))
    wire_ref[...] = wire


def back_kernel(wire_ref, owner_ref, rank_ref, out_ref):
    rows = out_ref.shape[1]
    got = jnp.zeros((LANES, LANES), F32)
    for piece in split3(wire_ref[...]):
        got = got + dot(piece, owner_ref[...], ((0,), (0,)))
    rank = rank_ref[0:1, :]
    change = jnp.zeros((rows, LANES), F32)
    for k in range(CAP):
        change = change + jnp.where(rank == k, got[k * rows : (k + 1) * rows], 0.0)
    out_ref[...] = jnp.broadcast_to(change[None], out_ref.shape)


def end_kernel(change_ref, up_ref, out_ref):
    levels, gcm = up_ref.shape
    half = change_ref.shape[0] // 2
    for f in range(2):
        tend = lax.dot_general(
            up_ref[...], change_ref[f * half : f * half + levels], (((0,), (0,)), ((), ())),
            precision=HI, preferred_element_type=F32,
        ) * (1.0 / (CX * SUB))
        out_ref[f * gcm : (f + 1) * gcm] = tend.astype(BF16)


VM = pl.BlockSpec(memory_space=pltpu.VMEM)
SM = pl.BlockSpec(memory_space=pltpu.SMEM)


def call(kernel, shapes, specs, *args, scratch=()):
    out = [jax.ShapeDtypeStruct(s, d) for s, d in shapes]
    many = len(out) > 1
    return pl.pallas_call(
        kernel,
        out_shape=out if many else out[0],
        in_specs=specs,
        out_specs=[VM] * len(out) if many else VM,
        scratch_shapes=list(scratch),
    )(*args)


def shards(gcm_state, crm_state, courant, cloud_mask, level_down, level_up, column_map):
    peers = lax.axis_size("wide")
    ring = lax.axis_size("narrow")
    columns, width = gcm_state.shape
    levels = crm_state.shape[1]
    own = crm_state.shape[2]
    w = lax.axis_index("wide").astype(jnp.int32).reshape(1)
    targets = column_map.reshape(peers, columns)
    n = peers * ROWS

    wire, owner, send_rank = call(
        pack_kernel,
        [((n, LANES), BF16), ((peers, LANES), BF16), ((8, LANES), jnp.int32)],
        [SM, VM, VM], w, targets, gcm_state.T,
    )
    arrived = lax.all_to_all(
        wire.reshape(n // 2, 2, LANES), "wide", split_axis=0, concat_axis=0, tiled=True
    ).reshape(n, LANES)

    forward = [(i, (i + 1) % ring) for i in range(ring)]
    backward = [(b, a) for a, b in forward]
    low = lax.ppermute(crm_state[:, :, own - SUB :], "narrow", forward)
    high = lax.ppermute(crm_state[:, :, :SUB], "narrow", backward)

    slots, take, take_rank = call(
        route_kernel,
        [((peers, CAP * LANES), BF16), ((n, 2 * LANES), BF16), ((8, LANES), jnp.int32)],
        [SM, VM], w, targets,
    )
    started = call(
        start_kernel, [((2, levels, own + 2 * SUB, LANES), F32)], [VM] * 4,
        crm_state, low, high, courant,
    )
    crm_new, diff = call(
        main_kernel,
        [((2, levels, own, LANES), BF16), ((2, ring * 4, LANES), F32)],
        [VM] * 8,
        arrived, take, take_rank, started, crm_state, courant, cloud_mask, level_down,
        scratch=[
            pltpu.VMEM((2, ring * 4, LANES), F32),
            pltpu.VMEM((levels, LANES), F32),
            pltpu.VMEM((2, levels, own + 2 * SUB, LANES), F32),
        ],
    )
    parts = lax.all_to_all(
        diff.reshape(ring, 8, LANES), "narrow", split_axis=0, concat_axis=0, tiled=True
    )
    back = call(turn_kernel, [((peers, LANES), F32)], [VM] * 2, parts, slots)
    back = lax.all_to_all(
        back.reshape(peers, 1, LANES), "wide", split_axis=0, concat_axis=0, tiled=True
    ).reshape(peers, LANES)
    change = call(back_kernel, [((ring, 8, LANES), F32)], [VM] * 3, back, owner, send_rank)
    change = lax.all_to_all(change, "narrow", split_axis=0, concat_axis=0, tiled=True)
    tendency = call(
        end_kernel, [((width, LANES), BF16)], [VM] * 2,
        change.reshape(ring * 8, LANES), level_up.T,
    )
    return tendency.T, crm_new


def solution(mesh):
    placed = (
        P("wide", None),
        P(None, None, "narrow", "wide"),
        P(None, "wide"),
        P(None, "wide"),
        P(),
        P(),
        P(),
    )
    return jax.shard_map(
        shards,
        mesh=mesh,
        in_specs=placed,
        out_specs=(P("wide", None), P(None, None, "narrow", "wide")),
        check_vma=False,
    )
```

```python
import jax
import jax.numpy as jnp
from jax import lax
from jax.experimental import pallas as pl
from jax.experimental.pallas import tpu as pltpu
from jax.sharding import PartitionSpec as P


CX = 256
SUB = 4
CAP = 4
ROWS = 6
LANES = 128
EXTRA = 16
NEAR = 4
HI = lax.Precision.HIGHEST
F32 = jnp.float32
BF16 = jnp.bfloat16


def iota(shape, dim):
    return lax.broadcasted_iota(jnp.int32, shape, dim)


def dot(a, b, dims):
    return lax.dot_general(a, b, (dims, ((), ())), preferred_element_type=F32)


def split3(x):
    a = x.astype(BF16)
    r = x - a.astype(F32)
    b = r.astype(BF16)
    c = (r - b.astype(F32)).astype(BF16)
    return a, b, c


def row_parts(n):
    row = iota((n, LANES), 0)
    peer = (row * 10923) >> 16
    return peer, row - peer * ROWS


def before_matrix():
    return (iota((LANES, LANES), 0) < iota((LANES, LANES), 1)).astype(BF16)


def pack_kernel(
    w_ref, map_hbm, state_hbm, crm_hbm, courant_hbm, mask_hbm, down_hbm, up_hbm,
    wire_ref, owner_ref, rank_ref, first_ref, last_ref,
    map_ref, crm_ref, courant_ref, mask_ref, down_ref, up_ref,
    state_ref, sems,
):
    pairs = (
        (map_hbm, map_ref), (state_hbm, state_ref), (crm_hbm, crm_ref), (courant_hbm, courant_ref),
        (mask_hbm, mask_ref), (down_hbm, down_ref), (up_hbm, up_ref),
    )
    copies = [pltpu.make_async_copy(a, b, sems.at[i]) for i, (a, b) in enumerate(pairs)]
    for copy in copies:
        copy.start()
    copies[0].wait()
    peers = map_ref.shape[0]
    mine = map_ref[pl.ds(w_ref[0], 1), :] >> 7
    own = iota((peers, LANES), 0) == mine
    own_b = own.astype(BF16)
    count = dot(own_b, before_matrix(), ((1,), (0,)))
    rank = jnp.sum(jnp.where(own, count, 0.0), axis=0, keepdims=True).astype(jnp.int32)
    owner_ref[...] = own_b
    rank_ref[...] = jnp.broadcast_to(rank, rank_ref.shape)
    n = peers * ROWS
    peer, part = row_parts(n)
    to_peer = peer == mine
    main = (to_peer & (part == rank)).astype(BF16)
    tail = (to_peer & (part == CAP)).astype(BF16)
    copies[1].wait()
    state = state_ref[...].astype(BF16)
    levels = state.shape[0]
    extra = state[LANES:levels].astype(F32)
    spread = [jnp.where(rank == k, extra, 0.0) for k in range(CAP)]
    spread.append(jnp.zeros((LANES - CAP * EXTRA, LANES), F32))
    spread = jnp.concatenate(spread, axis=0).astype(BF16)
    wire = dot(main, state[:LANES], ((1,), (1,))) + dot(tail, spread, ((1,), (1,)))
    wire_ref[...] = wire.astype(BF16)
    copies[2].wait()
    own_columns = crm_ref.shape[2]
    first_ref[...] = crm_ref[:, :, :SUB]
    last_ref[...] = crm_ref[:, :, own_columns - SUB :]
    for copy in copies[3:]:
        copy.wait()


def route_kernel(w_ref, map_ref, slot_ref, take_ref, rank_ref):
    peers = map_ref.shape[0]
    targets = map_ref[...]
    here = (targets >> 7) == w_ref[0]
    local = (targets & (LANES - 1)).astype(F32) + 1.0
    count = dot(here.astype(BF16), before_matrix(), ((1,), (0,)))
    slots = []
    lane = iota((peers, LANES), 1).astype(F32) + 1.0
    for k in range(CAP):
        hit = here & (count == float(k))
        one = jnp.sum(jnp.where(hit, local, 0.0), axis=1, keepdims=True)
        slots.append((one == lane).astype(F32))
    rank = jnp.zeros((1, LANES), F32)
    anyslot = jnp.zeros((peers, LANES), F32)
    for k in range(CAP):
        rank = rank + float(k) * jnp.sum(slots[k], axis=0, keepdims=True)
        anyslot = anyslot + slots[k]
        slot_ref[:, k * LANES : (k + 1) * LANES] = slots[k].astype(BF16)
    rank_ref[...] = jnp.broadcast_to(rank, rank_ref.shape).astype(jnp.int32)
    n = peers * ROWS
    row = iota((n, peers), 0)
    peer = (row * 10923) >> 16
    part = row - peer * ROWS
    same = peer == iota((n, peers), 1)
    main = jnp.zeros((n, LANES), F32)
    for k in range(CAP):
        main = main + dot((same & (part == k)).astype(BF16), slots[k].astype(BF16), ((1,), (0,)))
    tail = dot((same & (part == CAP)).astype(BF16), anyslot.astype(BF16), ((1,), (0,)))
    take_ref[:, :LANES] = main.astype(BF16)
    take_ref[:, LANES:] = tail.astype(BF16)


def horizontal(x, a0, a1, keep=None):
    n = x.shape[0]
    left = pltpu.roll(x, 1, 0)
    right = pltpu.roll(x, n - 1, 0)
    if keep is not None:
        left, x, right = left[:keep], x[:keep], right[:keep]
    return a1 * left + a0 * x + 0.15 * right


def start_kernel(crm_ref, low_ref, high_ref, courant_ref, out_ref):
    levels = crm_ref.shape[1]

    def mixed(level):
        c = courant_ref[pl.ds(level, 1), :]
        a0, a1 = 0.7 - c, c + 0.15
        result = []
        for f in range(2):
            x = jnp.concatenate(
                [
                    crm_ref[f, level].astype(F32),
                    high_ref[f, level].astype(F32),
                    low_ref[f, level].astype(F32),
                ],
                axis=0,
            )
            result.append(horizontal(x, a0, a1))
        return tuple(result)

    def body(level, carry):
        below, here = carry
        above = mixed(jnp.minimum(level + 1, levels - 1))
        for f in range(2):
            out_ref[f, level] = 0.8 * here[f] + 0.1 * (above[f] + below[f])
        return here, above

    first = mixed(0)
    lax.fori_loop(0, levels, body, (first, first), unroll=4)


def main_kernel(
    wire_ref, take_ref, rank_ref, start_ref, crm_ref, courant_ref, mask_ref, down_ref,
    new_ref, diff_ref, force_ref, cloud_ref, field_ref,
):
    levels = crm_ref.shape[1]
    gcm = down_ref.shape[1]
    own = crm_ref.shape[2]
    got = dot(wire_ref[...], take_ref[...], ((0,), (0,)))
    tail = jnp.zeros((EXTRA, LANES), F32)
    rank = rank_ref[0:1, :]
    for k in range(CAP):
        tail = tail + jnp.where(rank == k, got[k * EXTRA : (k + 1) * EXTRA, LANES:], 0.0)
    rows = jnp.concatenate([got[:, :LANES], tail], axis=0)
    for f in range(2):
        force = lax.dot_general(
            down_ref[...], rows[f * gcm : (f + 1) * gcm], (((1,), (0,)), ((), ())),
            precision=HI, preferred_element_type=F32,
        )
        force_ref[f, :levels] = 0.25 * force
    cloud_ref[...] = mask_ref[...].astype(F32) * 0.3
    diff_ref[...] = jnp.zeros_like(diff_ref)

    def physics(pair, level):
        t = pair[0] + force_ref[0, pl.ds(level, 1), :]
        q = pair[1] + force_ref[1, pl.ds(level, 1), :]
        condensed = cloud_ref[pl.ds(level, 1), :] * jnp.maximum(q, 0.0)
        return t + 2.0 * condensed, q - condensed

    def substep(index):
        source = start_ref if index == 1 else field_ref
        last = index == SUB - 1
        keep = own if last else None

        def mixed(level):
            c = courant_ref[pl.ds(level, 1), :]
            a0, a1 = 0.7 - c, c + 0.15
            pair = (source[0, level], source[1, level])
            if index == 1:
                pair = physics(pair, level)
            return tuple(horizontal(x, a0, a1, keep) for x in pair)

        def body(level, carry):
            below, here = carry
            above = mixed(jnp.minimum(level + 1, levels - 1))
            pair = tuple(0.8 * here[f] + 0.1 * (above[f] + below[f]) for f in range(2))
            pair = physics(pair, level)
            for f in range(2):
                if last:
                    new_ref[f, level] = pair[f].astype(BF16)
                    change = pair[f] - crm_ref[f, level].astype(F32)
                    diff_ref[f, pl.ds(level, 1), :] = jnp.sum(change, axis=0, keepdims=True)
                else:
                    field_ref[f, level] = pair[f]
            return here, above

        first = mixed(0)
        lax.fori_loop(0, levels, body, (first, first), unroll=4)

    for index in range(1, SUB):
        substep(index)


def turn_kernel(part_ref, slot_ref, wire_ref):
    total = jnp.sum(part_ref[...], axis=0)
    peers = wire_ref.shape[0]
    rows = total.shape[0]
    wire = jnp.zeros((peers, LANES), F32)
    for piece in split3(total):
        for k in range(CAP):
            padded = []
            if k:
                padded.append(jnp.zeros((k * rows, LANES), F32))
            padded.append(piece.astype(F32))
            if (k + 1) * rows < LANES:
                padded.append(jnp.zeros((LANES - (k + 1) * rows, LANES), F32))
            block = jnp.concatenate(padded, axis=0).astype(BF16)
            wire = wire + dot(slot_ref[:, k * LANES : (k + 1) * LANES], block, ((1,), (1,)))
    wire_ref[...] = wire


def back_kernel(wire_ref, owner_ref, rank_ref, out_ref):
    rows = out_ref.shape[1]
    got = jnp.zeros((LANES, LANES), F32)
    for piece in split3(wire_ref[...]):
        got = got + dot(piece, owner_ref[...], ((0,), (0,)))
    rank = rank_ref[0:1, :]
    change = jnp.zeros((rows, LANES), F32)
    for k in range(CAP):
        change = change + jnp.where(rank == k, got[k * rows : (k + 1) * rows], 0.0)
    out_ref[...] = jnp.broadcast_to(change[None], out_ref.shape)


def end_kernel(part_ref, up_ref, out_ref):
    levels, gcm = up_ref.shape
    ring, _, _ = part_ref.shape
    pieces = []
    for c in range(NEAR):
        piece = part_ref[c]
        for g in range(NEAR + c, ring, NEAR):
            piece = piece + part_ref[g]
        pieces.append(piece)
    change = jnp.concatenate(pieces, axis=0)
    half = change.shape[0] // 2
    for f in range(2):
        tend = lax.dot_general(
            up_ref[...], change[f * half : f * half + levels], (((0,), (0,)), ((), ())),
            precision=HI, preferred_element_type=F32,
        ) * (1.0 / (CX * SUB))
        out_ref[f * gcm : (f + 1) * gcm] = tend.astype(BF16)


VM = pl.BlockSpec(memory_space=pltpu.VMEM)
SM = pl.BlockSpec(memory_space=pltpu.SMEM)
HB = pl.BlockSpec(memory_space=pltpu.HBM)


def call(kernel, shapes, specs, *args, scratch=(), room=4):
    out = [jax.ShapeDtypeStruct(s, d) for s, d in shapes]
    many = len(out) > 1
    return pl.pallas_call(
        kernel,
        out_shape=out if many else out[0],
        in_specs=specs,
        out_specs=[VM] * len(out) if many else VM,
        scratch_shapes=list(scratch),
        compiler_params=pltpu.CompilerParams(vmem_limit_bytes=room << 20),
    )(*args)


def shards(gcm_state, crm_state, courant, cloud_mask, level_down, level_up, column_map):
    peers = lax.axis_size("wide")
    ring = lax.axis_size("narrow")
    columns, width = gcm_state.shape
    levels = crm_state.shape[1]
    own = crm_state.shape[2]
    w = lax.axis_index("wide").astype(jnp.int32).reshape(1)
    targets = column_map.reshape(peers, columns)
    n = peers * ROWS
    near = [[g * NEAR + i for i in range(NEAR)] for g in range(ring // NEAR)]
    forward = [(i, (i + 1) % ring) for i in range(ring)]
    backward = [(b, a) for a, b in forward]
    args = (targets, gcm_state.T, crm_state, courant, cloud_mask, level_down, level_up.T)
    resident = [(x.shape, x.dtype) for x in args]

    wire, owner, send_rank, first, last, targets, crm, courant, cloud_mask, down, up = call(
        pack_kernel,
        [((n, LANES), BF16), ((peers, LANES), BF16), ((8, LANES), jnp.int32)]
        + [((2, levels, SUB, LANES), BF16)] * 2
        + resident[:1] + resident[2:],
        [SM] + [HB] * 7, w, *[pltpu.with_memory_space_constraint(x, pltpu.HBM) for x in args],
        scratch=[pltpu.VMEM((width, LANES), F32), pltpu.SemaphoreType.DMA((7,))],
    )
    low = lax.ppermute(last, "narrow", forward)
    arrived = lax.all_to_all(
        wire.reshape(n // 2, 2, LANES), "wide", split_axis=0, concat_axis=0, tiled=True
    ).reshape(n, LANES)
    high = lax.ppermute(first, "narrow", backward)

    slots, take, take_rank = call(
        route_kernel,
        [((peers, CAP * LANES), BF16), ((n, 2 * LANES), BF16), ((8, LANES), jnp.int32)],
        [SM, VM], w, targets,
    )
    started = call(
        start_kernel, [((2, levels, own + 2 * SUB, LANES), F32)], [VM] * 4,
        crm, low, high, courant,
    )
    crm_new, diff = call(
        main_kernel,
        [((2, levels, own, LANES), BF16), ((2, ring * 4, LANES), F32)],
        [VM] * 8,
        arrived, take, take_rank, started, crm, courant, cloud_mask, down,
        scratch=[
            pltpu.VMEM((2, ring * 4, LANES), F32),
            pltpu.VMEM((levels, LANES), F32),
            pltpu.VMEM((2, levels, own + 2 * SUB, LANES), F32),
        ],
        room=8,
    )
    rows = 2 * ring * 4 // NEAR
    parts = lax.all_to_all(
        diff.reshape(NEAR, rows, LANES), "narrow", split_axis=0, concat_axis=0,
        axis_index_groups=near, tiled=True,
    )
    back = call(turn_kernel, [((peers, LANES), F32)], [VM] * 2, parts, slots)
    back = lax.all_to_all(
        back.reshape(peers, 1, LANES), "wide", split_axis=0, concat_axis=0, tiled=True
    ).reshape(peers, LANES)
    change = call(back_kernel, [((ring, rows, LANES), F32)], [VM] * 3, back, owner, send_rank)
    change = lax.all_to_all(change, "narrow", split_axis=0, concat_axis=0, tiled=True)
    tendency = call(end_kernel, [((width, LANES), BF16)], [VM] * 2, change, up)
    return tendency.T, crm_new


def solution(mesh):
    placed = (
        P("wide", None),
        P(None, None, "narrow", "wide"),
        P(None, "wide"),
        P(None, "wide"),
        P(),
        P(),
        P(),
    )

    return jax.shard_map(
        shards,
        mesh=mesh,
        in_specs=placed,
        out_specs=(P("wide", None), P(None, None, "narrow", "wide")),
        check_vma=False,
    )
```

```python
import jax
import jax.numpy as jnp
from jax import lax
from jax.experimental import pallas as pl
from jax.experimental.pallas import tpu as pltpu
from jax.sharding import PartitionSpec as P


CX = 256
SUB = 4
CAP = 4
ROWS = 6
LANES = 128
EXTRA = 16
NEAR = 4
HI = lax.Precision.HIGHEST
F32 = jnp.float32
BF16 = jnp.bfloat16


def iota(shape, dim):
    return lax.broadcasted_iota(jnp.int32, shape, dim)


def dot(a, b, dims):
    return lax.dot_general(a, b, (dims, ((), ())), preferred_element_type=F32)


def split3(x):
    a = x.astype(BF16)
    r = x - a.astype(F32)
    b = r.astype(BF16)
    c = (r - b.astype(F32)).astype(BF16)
    return a, b, c


def row_parts(n):
    row = iota((n, LANES), 0)
    peer = (row * 10923) >> 16
    return peer, row - peer * ROWS


def before_matrix():
    return (iota((LANES, LANES), 0) < iota((LANES, LANES), 1)).astype(BF16)


def pack_kernel(
    w_ref, map_hbm, state_hbm, crm_hbm, courant_hbm, mask_hbm, down_hbm, up_hbm,
    wire_ref, owner_ref, rank_ref, first_ref, last_ref,
    map_ref, crm_ref, courant_ref, mask_ref, down_ref, up_ref,
    state_ref, sems,
):
    pairs = (
        (map_hbm, map_ref), (state_hbm, state_ref), (crm_hbm, crm_ref), (courant_hbm, courant_ref),
        (mask_hbm, mask_ref), (down_hbm, down_ref), (up_hbm, up_ref),
    )
    copies = [pltpu.make_async_copy(a, b, sems.at[i]) for i, (a, b) in enumerate(pairs)]
    for copy in copies:
        copy.start()
    copies[0].wait()
    peers = map_ref.shape[0]
    mine = map_ref[pl.ds(w_ref[0], 1), :] >> 7
    own = iota((peers, LANES), 0) == mine
    own_b = own.astype(BF16)
    count = dot(own_b, before_matrix(), ((1,), (0,)))
    rank = jnp.sum(jnp.where(own, count, 0.0), axis=0, keepdims=True).astype(jnp.int32)
    owner_ref[...] = own_b
    rank_ref[...] = jnp.broadcast_to(rank, rank_ref.shape)
    n = peers * ROWS
    peer, part = row_parts(n)
    to_peer = peer == mine
    main = (to_peer & (part == rank)).astype(BF16)
    tail = (to_peer & (part == CAP)).astype(BF16)
    copies[1].wait()
    state = state_ref[...].astype(BF16)
    levels = state.shape[0]
    extra = state[LANES:levels].astype(F32)
    spread = [jnp.where(rank == k, extra, 0.0) for k in range(CAP)]
    spread.append(jnp.zeros((LANES - CAP * EXTRA, LANES), F32))
    spread = jnp.concatenate(spread, axis=0).astype(BF16)
    wire = dot(main, state[:LANES], ((1,), (1,))) + dot(tail, spread, ((1,), (1,)))
    wire_ref[...] = wire.astype(BF16)
    copies[2].wait()
    own_columns = crm_ref.shape[2]
    first_ref[...] = crm_ref[:, :, :SUB]
    last_ref[...] = crm_ref[:, :, own_columns - SUB :]
    for copy in copies[3:]:
        copy.wait()


def route_kernel(w_ref, map_ref, slot_ref, take_ref, rank_ref):
    peers = map_ref.shape[0]
    targets = map_ref[...]
    here = (targets >> 7) == w_ref[0]
    local = (targets & (LANES - 1)).astype(F32) + 1.0
    count = dot(here.astype(BF16), before_matrix(), ((1,), (0,)))
    slots = []
    lane = iota((peers, LANES), 1).astype(F32) + 1.0
    for k in range(CAP):
        hit = here & (count == float(k))
        one = jnp.sum(jnp.where(hit, local, 0.0), axis=1, keepdims=True)
        slots.append((one == lane).astype(F32))
    rank = jnp.zeros((1, LANES), F32)
    anyslot = jnp.zeros((peers, LANES), F32)
    for k in range(CAP):
        rank = rank + float(k) * jnp.sum(slots[k], axis=0, keepdims=True)
        anyslot = anyslot + slots[k]
        slot_ref[:, k * LANES : (k + 1) * LANES] = slots[k].astype(BF16)
    rank_ref[...] = jnp.broadcast_to(rank, rank_ref.shape).astype(jnp.int32)
    n = peers * ROWS
    row = iota((n, peers), 0)
    peer = (row * 10923) >> 16
    part = row - peer * ROWS
    same = peer == iota((n, peers), 1)
    main = jnp.zeros((n, LANES), F32)
    for k in range(CAP):
        main = main + dot((same & (part == k)).astype(BF16), slots[k].astype(BF16), ((1,), (0,)))
    tail = dot((same & (part == CAP)).astype(BF16), anyslot.astype(BF16), ((1,), (0,)))
    take_ref[:, :LANES] = main.astype(BF16)
    take_ref[:, LANES:] = tail.astype(BF16)


def horizontal(x, a0, a1, keep=None):
    n = x.shape[0]
    left = pltpu.roll(x, 1, 0)
    right = pltpu.roll(x, n - 1, 0)
    if keep is not None:
        left, x, right = left[:keep], x[:keep], right[:keep]
    return a1 * left + a0 * x + 0.15 * right


def start_kernel(crm_ref, low_ref, high_ref, courant_ref, out_ref):
    levels = crm_ref.shape[1]

    def mixed(level):
        c = courant_ref[pl.ds(level, 1), :]
        a0, a1 = 0.7 - c, c + 0.15
        result = []
        for f in range(2):
            x = jnp.concatenate(
                [
                    crm_ref[f, level].astype(F32),
                    high_ref[f, level].astype(F32),
                    low_ref[f, level].astype(F32),
                ],
                axis=0,
            )
            result.append(horizontal(x, a0, a1))
        return tuple(result)

    def body(level, carry):
        below, here = carry
        above = mixed(jnp.minimum(level + 1, levels - 1))
        for f in range(2):
            out_ref[f, level] = 0.8 * here[f] + 0.1 * (above[f] + below[f])
        return here, above

    first = mixed(0)
    lax.fori_loop(0, levels, body, (first, first), unroll=4)


def main_kernel(
    wire_ref, take_ref, rank_ref, start_ref, crm_ref, courant_ref, mask_ref, down_ref,
    new_ref, diff_ref, force_ref, cloud_ref, field_ref,
):
    levels = crm_ref.shape[1]
    gcm = down_ref.shape[1]
    own = crm_ref.shape[2]
    got = dot(wire_ref[...], take_ref[...], ((0,), (0,)))
    tail = jnp.zeros((EXTRA, LANES), F32)
    rank = rank_ref[0:1, :]
    for k in range(CAP):
        tail = tail + jnp.where(rank == k, got[k * EXTRA : (k + 1) * EXTRA, LANES:], 0.0)
    rows = jnp.concatenate([got[:, :LANES], tail], axis=0)
    for f in range(2):
        force = lax.dot_general(
            down_ref[...], rows[f * gcm : (f + 1) * gcm], (((1,), (0,)), ((), ())),
            precision=HI, preferred_element_type=F32,
        )
        force_ref[f, :levels] = 0.25 * force
    cloud_ref[...] = mask_ref[...].astype(F32) * 0.3
    diff_ref[...] = jnp.zeros_like(diff_ref)

    def physics(pair, level):
        t = pair[0] + force_ref[0, pl.ds(level, 1), :]
        q = pair[1] + force_ref[1, pl.ds(level, 1), :]
        condensed = cloud_ref[pl.ds(level, 1), :] * jnp.maximum(q, 0.0)
        return t + 2.0 * condensed, q - condensed

    def substep(index):
        source = start_ref if index == 1 else field_ref
        last = index == SUB - 1
        keep = own if last else None

        def mixed(level):
            c = courant_ref[pl.ds(level, 1), :]
            a0, a1 = 0.7 - c, c + 0.15
            pair = (source[0, level], source[1, level])
            if index == 1:
                pair = physics(pair, level)
            return tuple(horizontal(x, a0, a1, keep) for x in pair)

        def body(level, carry):
            below, here = carry
            above = mixed(jnp.minimum(level + 1, levels - 1))
            pair = tuple(0.8 * here[f] + 0.1 * (above[f] + below[f]) for f in range(2))
            pair = physics(pair, level)
            for f in range(2):
                if last:
                    new_ref[f, level] = pair[f].astype(BF16)
                    change = pair[f] - crm_ref[f, level].astype(F32)
                    diff_ref[f, pl.ds(level, 1), :] = jnp.sum(change, axis=0, keepdims=True)
                else:
                    field_ref[f, level] = pair[f]
            return here, above

        first = mixed(0)
        lax.fori_loop(0, levels, body, (first, first), unroll=4)

    for index in range(1, SUB):
        substep(index)


def turn_kernel(part_ref, slot_ref, wire_ref):
    total = jnp.sum(part_ref[...], axis=0)
    peers = wire_ref.shape[0]
    rows = total.shape[0]
    wire = jnp.zeros((peers, LANES), F32)
    for piece in split3(total):
        for k in range(CAP):
            padded = []
            if k:
                padded.append(jnp.zeros((k * rows, LANES), F32))
            padded.append(piece.astype(F32))
            if (k + 1) * rows < LANES:
                padded.append(jnp.zeros((LANES - (k + 1) * rows, LANES), F32))
            block = jnp.concatenate(padded, axis=0).astype(BF16)
            wire = wire + dot(slot_ref[:, k * LANES : (k + 1) * LANES], block, ((1,), (1,)))
    wire_ref[...] = wire


def back_kernel(wire_ref, owner_ref, rank_ref, out_ref):
    rows = out_ref.shape[1]
    got = jnp.zeros((LANES, LANES), F32)
    for piece in split3(wire_ref[...]):
        got = got + dot(piece, owner_ref[...], ((0,), (0,)))
    rank = rank_ref[0:1, :]
    change = jnp.zeros((rows, LANES), F32)
    for k in range(CAP):
        change = change + jnp.where(rank == k, got[k * rows : (k + 1) * rows], 0.0)
    out_ref[...] = jnp.broadcast_to(change[None], out_ref.shape)


def sum_kernel(part_ref, out_ref):
    out_ref[...] = jnp.broadcast_to(jnp.sum(part_ref[...], axis=0)[None], out_ref.shape)


def end_kernel(change_ref, up_ref, out_ref):
    levels, gcm = up_ref.shape
    half = change_ref.shape[0] // 2
    for f in range(2):
        tend = lax.dot_general(
            up_ref[...], change_ref[f * half : f * half + levels], (((0,), (0,)), ((), ())),
            precision=HI, preferred_element_type=F32,
        ) * (1.0 / (CX * SUB))
        out_ref[f * gcm : (f + 1) * gcm] = tend.astype(BF16)


VM = pl.BlockSpec(memory_space=pltpu.VMEM)
SM = pl.BlockSpec(memory_space=pltpu.SMEM)
HB = pl.BlockSpec(memory_space=pltpu.HBM)


def call(kernel, shapes, specs, *args, scratch=(), room=4):
    out = [jax.ShapeDtypeStruct(s, d) for s, d in shapes]
    many = len(out) > 1
    return pl.pallas_call(
        kernel,
        out_shape=out if many else out[0],
        in_specs=specs,
        out_specs=[VM] * len(out) if many else VM,
        scratch_shapes=list(scratch),
        compiler_params=pltpu.CompilerParams(vmem_limit_bytes=room << 20),
    )(*args)


def shards(gcm_state, crm_state, courant, cloud_mask, level_down, level_up, column_map):
    peers = lax.axis_size("wide")
    ring = lax.axis_size("narrow")
    columns, width = gcm_state.shape
    levels = crm_state.shape[1]
    own = crm_state.shape[2]
    w = lax.axis_index("wide").astype(jnp.int32).reshape(1)
    targets = column_map.reshape(peers, columns)
    n = peers * ROWS
    near = [[g * NEAR + i for i in range(NEAR)] for g in range(ring // NEAR)]
    far = [[g + NEAR * i for i in range(ring // NEAR)] for g in range(NEAR)]
    forward = [(i, (i + 1) % ring) for i in range(ring)]
    backward = [(b, a) for a, b in forward]
    args = (targets, gcm_state.T, crm_state, courant, cloud_mask, level_down, level_up.T)
    resident = [(x.shape, x.dtype) for x in args]

    wire, owner, send_rank, first, last, targets, crm, courant, cloud_mask, down, up = call(
        pack_kernel,
        [((n, LANES), BF16), ((peers, LANES), BF16), ((8, LANES), jnp.int32)]
        + [((2, levels, SUB, LANES), BF16)] * 2
        + resident[:1] + resident[2:],
        [SM] + [HB] * 7, w, *[pltpu.with_memory_space_constraint(x, pltpu.HBM) for x in args],
        scratch=[pltpu.VMEM((width, LANES), F32), pltpu.SemaphoreType.DMA((7,))],
    )
    high = lax.ppermute(first, "narrow", backward)
    arrived = lax.all_to_all(
        wire.reshape(n // 2, 2, LANES), "wide", split_axis=0, concat_axis=0, tiled=True
    ).reshape(n, LANES)
    low = lax.ppermute(last, "narrow", forward)

    slots, take, take_rank = call(
        route_kernel,
        [((peers, CAP * LANES), BF16), ((n, 2 * LANES), BF16), ((8, LANES), jnp.int32)],
        [SM, VM], w, targets,
    )
    started = call(
        start_kernel, [((2, levels, own + 2 * SUB, LANES), F32)], [VM] * 4,
        crm, low, high, courant,
    )
    crm_new, diff = call(
        main_kernel,
        [((2, levels, own, LANES), BF16), ((2, ring * 4, LANES), F32)],
        [VM] * 8,
        arrived, take, take_rank, started, crm, courant, cloud_mask, down,
        scratch=[
            pltpu.VMEM((2, ring * 4, LANES), F32),
            pltpu.VMEM((levels, LANES), F32),
            pltpu.VMEM((2, levels, own + 2 * SUB, LANES), F32),
        ],
        room=8,
    )
    rows = 2 * ring * 4 // NEAR
    parts = lax.all_to_all(
        diff.reshape(NEAR, rows, LANES), "narrow", split_axis=0, concat_axis=0,
        axis_index_groups=near, tiled=True,
    )
    back = call(turn_kernel, [((peers, LANES), F32)], [VM] * 2, parts, slots)
    back = lax.all_to_all(
        back.reshape(peers, 1, LANES), "wide", split_axis=0, concat_axis=0, tiled=True
    ).reshape(peers, LANES)
    change = call(back_kernel, [((NEAR, rows, LANES), F32)], [VM] * 3, back, owner, send_rank)
    change = lax.all_to_all(
        change, "narrow", split_axis=0, concat_axis=0, axis_index_groups=far, tiled=True
    )
    change = call(sum_kernel, [((NEAR, rows, LANES), F32)], [VM], change)
    change = lax.all_to_all(
        change, "narrow", split_axis=0, concat_axis=0, axis_index_groups=near, tiled=True
    )
    tendency = call(
        end_kernel, [((width, LANES), BF16)], [VM] * 2, change.reshape(NEAR * rows, LANES), up
    )
    return tendency.T, crm_new


def solution(mesh):
    placed = (
        P("wide", None),
        P(None, None, "narrow", "wide"),
        P(None, "wide"),
        P(None, "wide"),
        P(),
        P(),
        P(),
    )

    return jax.shard_map(
        shards,
        mesh=mesh,
        in_specs=placed,
        out_specs=(P("wide", None), P(None, None, "narrow", "wide")),
        check_vma=False,
    )
```

```python
import jax
import jax.numpy as jnp
from jax import lax
from jax.experimental import pallas as pl
from jax.experimental.pallas import tpu as pltpu
from jax.sharding import PartitionSpec as P


CX = 256
SUB = 4
CAP = 4
ROWS = 6
LANES = 128
EXTRA = 16
NEAR = 4
SIDE = 0.15
STEP = 1.0 / (0.1 * SIDE)
PAD = 8
PIECES = 3
UNROLL = 5
HI = lax.Precision.HIGHEST
F32 = jnp.float32
BF16 = jnp.bfloat16


def iota(shape, dim):
    return lax.broadcasted_iota(jnp.int32, shape, dim)


def dot(a, b, dims):
    return lax.dot_general(a, b, (dims, ((), ())), preferred_element_type=F32)


def split3(x):
    a = x.astype(BF16)
    r = x - a.astype(F32)
    b = r.astype(BF16)
    c = (r - b.astype(F32)).astype(BF16)
    return a, b, c


def row_parts(start):
    row = iota((LANES, LANES), 0) + start
    peer = (row * 10923) >> 16
    return peer, row - peer * ROWS


def before_matrix():
    return (iota((LANES, LANES), 0) < iota((LANES, LANES), 1)).astype(BF16)


def pack_kernel(
    place_ref, map_hbm, state_hbm, crm_hbm, courant_hbm, mask_hbm, down_hbm, up_hbm,
    wire_ref, owner_ref, rank_ref, face_ref, other_ref,
    map_ref, crm_ref, courant_ref, mask_ref, down_ref, up_ref,
    state_ref, sems,
):
    pairs = (
        (map_hbm, map_ref), (state_hbm, state_ref), (crm_hbm, crm_ref), (courant_hbm, courant_ref),
        (mask_hbm, mask_ref), (down_hbm, down_ref), (up_hbm, up_ref),
    )
    copies = [pltpu.make_async_copy(a, b, sems.at[i]) for i, (a, b) in enumerate(pairs)]
    for copy in copies:
        copy.start()
    copies[0].wait()
    peers = map_ref.shape[0]
    mine = map_ref[pl.ds(place_ref[0], 1), :] >> 7
    own = iota((peers, LANES), 0) == mine
    own_b = own.astype(BF16)
    count = dot(own_b, before_matrix(), ((1,), (0,)))
    rank = jnp.sum(jnp.where(own, count, 0.0), axis=0, keepdims=True).astype(jnp.int32)
    owner_ref[...] = own_b
    rank_ref[...] = jnp.broadcast_to(rank, rank_ref.shape)
    copies[1].wait()
    state = state_ref[...].astype(BF16)
    levels = state.shape[0]
    extra = state[LANES:levels].astype(F32)
    spread = [jnp.where(rank == k, extra, 0.0) for k in range(CAP)]
    spread.append(jnp.zeros((LANES - CAP * EXTRA, LANES), F32))
    spread = jnp.concatenate(spread, axis=0).astype(BF16)
    for start in range(0, peers * ROWS, LANES):
        peer, part = row_parts(start)
        to_peer = peer == mine
        main = (to_peer & (part == rank)).astype(BF16)
        tail = (to_peer & (part == CAP)).astype(BF16)
        wire = dot(main, state[:LANES], ((1,), (1,))) + dot(tail, spread, ((1,), (1,)))
        wire_ref[start : start + LANES] = wire.astype(BF16)
    copies[2].wait()
    own_columns = crm_ref.shape[2]
    odd = (place_ref[1] & 1) == 1

    def faces(to_low, to_high):
        def body(level, carry):
            for f in range(2):
                to_low[f, level] = crm_ref[f, level, :SUB]
                to_high[f, level] = crm_ref[f, level, own_columns - SUB :]
            return carry

        lax.fori_loop(0, crm_ref.shape[1], body, 0, unroll=UNROLL)

    @pl.when(odd)
    def _():
        faces(face_ref, other_ref)

    @pl.when(jnp.logical_not(odd))
    def _():
        faces(other_ref, face_ref)

    for copy in copies[3:]:
        copy.wait()


def route_kernel(
    place_ref, map_ref, courant_ref, mask_ref, slot_ref, take_ref, rank_ref, left_ref, here_ref, cloud_ref
):
    left_ref[...] = courant_ref[...] * (1.0 / SIDE) + 1.0
    here_ref[...] = (0.7 - courant_ref[...]) * (1.0 / SIDE)
    cloud_ref[...] = mask_ref[...].astype(F32) * 0.3
    peers = map_ref.shape[0]
    targets = map_ref[...]
    here = (targets >> 7) == place_ref[0]
    local = (targets & (LANES - 1)).astype(F32) + 1.0
    count = dot(here.astype(BF16), before_matrix(), ((1,), (0,)))
    slots = []
    lane = iota((peers, LANES), 1).astype(F32) + 1.0
    for k in range(CAP):
        hit = here & (count == float(k))
        one = jnp.sum(jnp.where(hit, local, 0.0), axis=1, keepdims=True)
        slots.append((one == lane).astype(F32))
    rank = jnp.zeros((1, LANES), F32)
    anyslot = jnp.zeros((peers, LANES), F32)
    for k in range(CAP):
        rank = rank + float(k) * jnp.sum(slots[k], axis=0, keepdims=True)
        anyslot = anyslot + slots[k]
        slot_ref[:, k * LANES : (k + 1) * LANES] = slots[k].astype(BF16)
    rank_ref[...] = jnp.broadcast_to(rank, rank_ref.shape).astype(jnp.int32)
    n = peers * ROWS
    row = iota((n, peers), 0)
    peer = (row * 10923) >> 16
    part = row - peer * ROWS
    same = peer == iota((n, peers), 1)
    main = jnp.zeros((n, LANES), F32)
    for k in range(CAP):
        main = main + dot((same & (part == k)).astype(BF16), slots[k].astype(BF16), ((1,), (0,)))
    tail = dot((same & (part == CAP)).astype(BF16), anyslot.astype(BF16), ((1,), (0,)))
    take_ref[:, :LANES] = main.astype(BF16)
    take_ref[:, LANES:] = tail.astype(BF16)


def mix(ref, f, level, left, here, rows):
    return (
        left * ref[f, level, PAD - 1 : PAD - 1 + rows]
        + here * ref[f, level, PAD : PAD + rows]
        + ref[f, level, PAD + 1 : PAD + 1 + rows]
    )


def put(ref, f, level, x):
    n = x.shape[0]
    ref[f, level, PAD : PAD + n] = x
    ref[f, level, PAD - 1 : PAD] = x[n - 1 :]
    ref[f, level, PAD + n : PAD + n + 1] = x[:1]


def column(levels, mixed, keep):
    def body(level, carry):
        below, here = carry
        above = mixed(jnp.minimum(level + 1, levels - 1))
        keep(level, [8.0 * h + (a + b) for a, h, b in zip(above, here, below, strict=True)])
        return here, above

    start = mixed(0)
    return body, (start, start)


def start_kernel(place_ref, crm_ref, near_ref, far_ref, left_ref, here_ref, out_ref, load_ref):
    levels = crm_ref.shape[1]
    odd = (place_ref[1] & 1) == 1

    def load(level, carry):
        fields = []
        for f in range(2):
            near = near_ref[f, level].astype(F32)
            far = far_ref[f, level].astype(F32)
            halo = jnp.where(
                odd, jnp.concatenate([far, near], axis=0), jnp.concatenate([near, far], axis=0)
            )
            fields.append(jnp.concatenate([crm_ref[f, level].astype(F32), halo], axis=0))
        put(load_ref, 0, level, fields[0] + 2.0 * fields[1])
        put(load_ref, 1, level, fields[1])
        return carry

    lax.fori_loop(0, levels, load, 0, unroll=UNROLL)
    rows = out_ref.shape[2]

    def mixed(level):
        left, here = left_ref[pl.ds(level, 1), :], here_ref[pl.ds(level, 1), :]
        return tuple(mix(load_ref, f, level, left, here, rows) for f in range(2))

    def keep(level, pair):
        for f in range(2):
            out_ref[f, level] = pair[f]

    body, carry = column(levels, mixed, keep)
    lax.fori_loop(0, levels, body, carry, unroll=UNROLL)


def main_kernel(
    wire_ref, take_ref, rank_ref, start_ref, crm_ref, left_ref, here_ref, cloud_ref, down_ref,
    new_hbm, diff_ref, force_ref, field_ref, next_ref, new_ref, sems,
):
    levels = crm_ref.shape[1]
    gcm = down_ref.shape[1]
    own = crm_ref.shape[2]
    full = start_ref.shape[2]
    got = dot(wire_ref[...], take_ref[...], ((0,), (0,)))
    tail = jnp.zeros((EXTRA, LANES), F32)
    rank = rank_ref[0:1, :]
    for k in range(CAP):
        tail = tail + jnp.where(rank == k, got[k * EXTRA : (k + 1) * EXTRA, LANES:], 0.0)
    rows = jnp.concatenate([got[:, :LANES], tail], axis=0)
    force = [
        lax.dot_general(
            down_ref[...], rows[f * gcm : (f + 1) * gcm], (((1,), (0,)), ((), ())),
            precision=HI, preferred_element_type=F32,
        )
        for f in range(2)
    ]
    force[0] = force[0] + 2.0 * force[1]
    for index in range(SUB):
        for f in range(2):
            force_ref[index, f, :levels] = (0.25 * STEP ** (index + 1)) * force[f]
    diff_ref[:, levels:] = jnp.zeros((2, diff_ref.shape[1] - levels, LANES), F32)

    def physics(pair, level, index):
        m = pair[0] + force_ref[index, 0, pl.ds(level, 1), :]
        q = pair[1] + force_ref[index, 1, pl.ds(level, 1), :]
        return m, q - cloud_ref[pl.ds(level, 1), :] * jnp.maximum(q, 0.0)

    def first(level, carry):
        pair = physics((start_ref[0, level], start_ref[1, level]), level, 0)
        for f in range(2):
            put(field_ref, f, level, pair[f])
        return carry

    lax.fori_loop(0, levels, first, 0, unroll=UNROLL)
    piece = levels // PIECES
    copies = []
    for index in range(1, SUB):
        last = index == SUB - 1
        source, target = (field_ref, next_ref) if index % 2 else (next_ref, field_ref)
        size = own if last else full

        def mixed(level, source=source, size=size):
            left, here = left_ref[pl.ds(level, 1), :], here_ref[pl.ds(level, 1), :]
            return tuple(mix(source, f, level, left, here, size) for f in range(2))

        def keep(level, pair, index=index, last=last, target=target):
            pair = physics(pair, level, index)
            if not last:
                for f in range(2):
                    put(target, f, level, pair[f])
                return
            scale = STEP**-SUB
            q = scale * pair[1]
            t = scale * pair[0] - 2.0 * q
            for f, x in enumerate((t, q)):
                new_ref[f, level] = x.astype(BF16)
                change = x - crm_ref[f, level].astype(F32)
                diff_ref[f, pl.ds(level, 1), :] = jnp.sum(change, axis=0, keepdims=True)

        body, carry = column(levels, mixed, keep)
        if not last:
            lax.fori_loop(0, levels, body, carry, unroll=UNROLL)
            continue
        for part in range(PIECES):
            carry = lax.fori_loop(part * piece, (part + 1) * piece, body, carry, unroll=UNROLL)
            span = pl.ds(part * piece, piece)
            for f in range(2):
                copy = pltpu.make_async_copy(
                    new_ref.at[f, span], new_hbm.at[f, span], sems.at[2 * part + f]
                )
                copy.start()
                copies.append(copy)
    for copy in copies:
        copy.wait()


def turn_kernel(part_ref, slot_ref, wire_ref):
    total = jnp.sum(part_ref[...], axis=0)
    peers = wire_ref.shape[0]
    rows = total.shape[0]
    wire = jnp.zeros((peers, LANES), F32)
    for piece in split3(total):
        for k in range(CAP):
            padded = []
            if k:
                padded.append(jnp.zeros((k * rows, LANES), F32))
            padded.append(piece.astype(F32))
            if (k + 1) * rows < LANES:
                padded.append(jnp.zeros((LANES - (k + 1) * rows, LANES), F32))
            block = jnp.concatenate(padded, axis=0).astype(BF16)
            wire = wire + dot(slot_ref[:, k * LANES : (k + 1) * LANES], block, ((1,), (1,)))
    wire_ref[...] = wire


def back_kernel(wire_ref, owner_ref, rank_ref, out_ref):
    rows = out_ref.shape[1]
    got = jnp.zeros((LANES, LANES), F32)
    for piece in split3(wire_ref[...]):
        got = got + dot(piece, owner_ref[...], ((0,), (0,)))
    rank = rank_ref[0:1, :]
    change = jnp.zeros((rows, LANES), F32)
    for k in range(CAP):
        change = change + jnp.where(rank == k, got[k * rows : (k + 1) * rows], 0.0)
    out_ref[...] = jnp.broadcast_to(change[None], out_ref.shape)


def sum_kernel(part_ref, out_ref):
    out_ref[...] = jnp.broadcast_to(jnp.sum(part_ref[...], axis=0)[None], out_ref.shape)


def end_kernel(change_ref, up_ref, out_ref):
    levels, gcm = up_ref.shape
    half = change_ref.shape[0] // 2
    for f in range(2):
        tend = lax.dot_general(
            up_ref[...], change_ref[f * half : f * half + levels], (((0,), (0,)), ((), ())),
            precision=HI, preferred_element_type=F32,
        ) * (1.0 / (CX * SUB))
        out_ref[f * gcm : (f + 1) * gcm] = tend.astype(BF16)


VM = pl.BlockSpec(memory_space=pltpu.VMEM)
SM = pl.BlockSpec(memory_space=pltpu.SMEM)
HB = pl.BlockSpec(memory_space=pltpu.HBM)


def call(kernel, shapes, specs, *args, scratch=(), room=4, outs=None):
    out = [jax.ShapeDtypeStruct(s, d) for s, d in shapes]
    many = len(out) > 1
    return pl.pallas_call(
        kernel,
        out_shape=out if many else out[0],
        in_specs=specs,
        out_specs=outs or ([VM] * len(out) if many else VM),
        scratch_shapes=list(scratch),
        compiler_params=pltpu.CompilerParams(vmem_limit_bytes=room << 20),
    )(*args)


def shards(gcm_state, crm_state, courant, cloud_mask, level_down, level_up, column_map):
    peers = lax.axis_size("wide")
    ring = lax.axis_size("narrow")
    columns, width = gcm_state.shape
    levels = crm_state.shape[1]
    own = crm_state.shape[2]
    place = jnp.stack([lax.axis_index("wide"), lax.axis_index("narrow")]).astype(jnp.int32)
    targets = column_map.reshape(peers, columns)
    n = peers * ROWS
    near = [[g * NEAR + i for i in range(NEAR)] for g in range(ring // NEAR)]
    far = [[g + NEAR * i for i in range(ring // NEAR)] for g in range(NEAR)]
    pairs = [(i, i ^ 1) for i in range(ring)]
    other_pairs = [(i, ((i + 1) ^ 1) - 1) for i in range(ring)]
    other_pairs = [(a, b % ring) for a, b in other_pairs]
    args = (targets, gcm_state.T, crm_state, courant, cloud_mask, level_down, level_up.T)
    resident = [(x.shape, x.dtype) for x in args]

    wire, owner, send_rank, face, other, targets, crm, courant, cloud_mask, down, up = call(
        pack_kernel,
        [((n, LANES), BF16), ((peers, LANES), BF16), ((8, LANES), jnp.int32)]
        + [((2, levels, SUB, LANES), BF16)] * 2
        + resident[:1] + resident[2:],
        [SM] + [HB] * 7, place, *[pltpu.with_memory_space_constraint(x, pltpu.HBM) for x in args],
        scratch=[pltpu.VMEM((width, LANES), F32), pltpu.SemaphoreType.DMA((7,))],
    )
    arrived = lax.all_to_all(
        wire.reshape(n // 2, 2, LANES), "wide", split_axis=0, concat_axis=0, tiled=True
    ).reshape(n, LANES)
    halo_near = lax.ppermute(face, "narrow", pairs)
    halo_far = lax.ppermute(other, "narrow", other_pairs)

    slots, take, take_rank, left, here, cloud = call(
        route_kernel,
        [((peers, CAP * LANES), BF16), ((n, 2 * LANES), BF16), ((8, LANES), jnp.int32)]
        + [((levels, LANES), F32)] * 3,
        [SM] + [VM] * 3, place, targets, courant, cloud_mask,
    )
    full = own + 2 * SUB
    padded = full + 2 * PAD
    started = call(
        start_kernel, [((2, levels, full, LANES), F32)], [SM] + [VM] * 5,
        place, crm, halo_near, halo_far, left, here,
        scratch=[pltpu.VMEM((2, levels, padded, LANES), F32)],
        room=6,
    )
    crm_new, diff = call(
        main_kernel,
        [((2, levels, own, LANES), BF16), ((2, ring * 4, LANES), F32)],
        [VM] * 9,
        arrived, take, take_rank, started, crm, left, here, cloud, down,
        scratch=[
            pltpu.VMEM((SUB, 2, ring * 4, LANES), F32),
            pltpu.VMEM((2, levels, padded, LANES), F32),
            pltpu.VMEM((2, levels, padded, LANES), F32),
            pltpu.VMEM((2, levels, own, LANES), BF16),
            pltpu.SemaphoreType.DMA((2 * PIECES,)),
        ],
        room=12,
        outs=[HB, VM],
    )
    rows = 2 * ring * 4 // NEAR
    parts = lax.all_to_all(
        diff.reshape(NEAR, rows, LANES), "narrow", split_axis=0, concat_axis=0,
        axis_index_groups=near, tiled=True,
    )
    back = call(turn_kernel, [((peers, LANES), F32)], [VM] * 2, parts, slots)
    back = lax.all_to_all(
        back.reshape(peers, 1, LANES), "wide", split_axis=0, concat_axis=0, tiled=True
    ).reshape(peers, LANES)
    change = call(back_kernel, [((NEAR, rows, LANES), F32)], [VM] * 3, back, owner, send_rank)
    change = lax.all_to_all(
        change, "narrow", split_axis=0, concat_axis=0, axis_index_groups=far, tiled=True
    )
    change = call(sum_kernel, [((NEAR, rows, LANES), F32)], [VM], change)
    change = lax.all_to_all(
        change, "narrow", split_axis=0, concat_axis=0, axis_index_groups=near, tiled=True
    )
    tendency = call(
        end_kernel, [((width, LANES), BF16)], [VM] * 2, change.reshape(NEAR * rows, LANES), up
    )
    return tendency.T, crm_new


def solution(mesh):
    placed = (
        P("wide", None),
        P(None, None, "narrow", "wide"),
        P(None, "wide"),
        P(None, "wide"),
        P(),
        P(),
        P(),
    )

    return jax.shard_map(
        shards,
        mesh=mesh,
        in_specs=placed,
        out_specs=(P("wide", None), P(None, None, "narrow", "wide")),
        check_vma=False,
    )
```

```python
import jax
import jax.numpy as jnp
from jax import lax
from jax.experimental import pallas as pl
from jax.experimental.pallas import tpu as pltpu
from jax.sharding import PartitionSpec as P


CX = 256
SUB = 4
CAP = 4
ROWS = 6
LANES = 128
EXTRA = 16
NEAR = 4
SIDE = 0.15
STEP = 1.0 / (0.1 * SIDE)
PAD = 8
PIECES = 3
UNROLL = 5
HI = lax.Precision.HIGHEST
F32 = jnp.float32
BF16 = jnp.bfloat16


def iota(shape, dim):
    return lax.broadcasted_iota(jnp.int32, shape, dim)


def dot(a, b, dims):
    return lax.dot_general(a, b, (dims, ((), ())), preferred_element_type=F32)


def split3(x):
    a = x.astype(BF16)
    r = x - a.astype(F32)
    b = r.astype(BF16)
    c = (r - b.astype(F32)).astype(BF16)
    return a, b, c


def row_parts(start):
    row = iota((LANES, LANES), 0) + start
    peer = (row * 10923) >> 16
    return peer, row - peer * ROWS


def before_matrix():
    return (iota((LANES, LANES), 0) < iota((LANES, LANES), 1)).astype(BF16)


def pack_kernel(
    map_hbm, state_hbm, crm_hbm, courant_hbm, mask_hbm, down_hbm, up_hbm,
    wire_ref, owner_ref, rank_ref, face_ref, other_ref,
    map_ref, crm_ref, courant_ref, mask_ref, down_ref, up_ref,
    state_ref, sems,
):
    pairs = (
        (map_hbm, map_ref), (state_hbm, state_ref), (crm_hbm, crm_ref), (courant_hbm, courant_ref),
        (mask_hbm, mask_ref), (down_hbm, down_ref), (up_hbm, up_ref),
    )
    copies = [pltpu.make_async_copy(a, b, sems.at[i]) for i, (a, b) in enumerate(pairs)]
    for copy in copies:
        copy.start()
    copies[0].wait()
    peers = map_ref.shape[0]
    mine = map_ref[pl.ds(lax.axis_index("wide"), 1), :] >> 7
    own = iota((peers, LANES), 0) == mine
    own_b = own.astype(BF16)
    count = dot(own_b, before_matrix(), ((1,), (0,)))
    rank = jnp.sum(jnp.where(own, count, 0.0), axis=0, keepdims=True).astype(jnp.int32)
    owner_ref[...] = own_b
    rank_ref[...] = jnp.broadcast_to(rank, rank_ref.shape)
    copies[1].wait()
    state = state_ref[...].astype(BF16)
    levels = state.shape[0]
    extra = state[LANES:levels].astype(F32)
    spread = [jnp.where(rank == k, extra, 0.0) for k in range(CAP)]
    spread.append(jnp.zeros((LANES - CAP * EXTRA, LANES), F32))
    spread = jnp.concatenate(spread, axis=0).astype(BF16)
    for start in range(0, peers * ROWS, LANES):
        peer, part = row_parts(start)
        to_peer = peer == mine
        main = (to_peer & (part == rank)).astype(BF16)
        tail = (to_peer & (part == CAP)).astype(BF16)
        wire = dot(main, state[:LANES], ((1,), (1,))) + dot(tail, spread, ((1,), (1,)))
        wire_ref[start : start + LANES] = wire.astype(BF16)
    copies[2].wait()
    own_columns = crm_ref.shape[2]
    odd = (lax.axis_index("narrow") & 1) == 1

    def faces(to_low, to_high):
        def body(level, carry):
            for f in range(2):
                to_low[f, level] = crm_ref[f, level, :SUB]
                to_high[f, level] = crm_ref[f, level, own_columns - SUB :]
            return carry

        lax.fori_loop(0, crm_ref.shape[1], body, 0, unroll=UNROLL)

    @pl.when(odd)
    def _():
        faces(face_ref, other_ref)

    @pl.when(jnp.logical_not(odd))
    def _():
        faces(other_ref, face_ref)

    for copy in copies[3:]:
        copy.wait()


def route_kernel(
    map_ref, crm_ref, courant_ref, mask_ref,
    slot_ref, take_ref, rank_ref, left_ref, here_ref, cloud_ref, wide_ref,
):
    own = crm_ref.shape[2]

    def widen(level, carry):
        q = crm_ref[1, level].astype(F32)
        m = crm_ref[0, level].astype(F32) + 2.0 * q
        for f, x in enumerate((m, q)):
            wide_ref[f, level, PAD : PAD + own] = x
            wide_ref[f, level, PAD + own + 2 * SUB : PAD + own + 2 * SUB + 1] = x[:1]
        return carry

    lax.fori_loop(0, crm_ref.shape[1], widen, 0, unroll=UNROLL)
    left_ref[...] = courant_ref[...] * (1.0 / SIDE) + 1.0
    here_ref[...] = (0.7 - courant_ref[...]) * (1.0 / SIDE)
    cloud_ref[...] = mask_ref[...].astype(F32) * 0.3
    peers = map_ref.shape[0]
    targets = map_ref[...]
    here = (targets >> 7) == lax.axis_index("wide")
    local = (targets & (LANES - 1)).astype(F32) + 1.0
    count = dot(here.astype(BF16), before_matrix(), ((1,), (0,)))
    slots = []
    lane = iota((peers, LANES), 1).astype(F32) + 1.0
    for k in range(CAP):
        hit = here & (count == float(k))
        one = jnp.sum(jnp.where(hit, local, 0.0), axis=1, keepdims=True)
        slots.append((one == lane).astype(F32))
    rank = jnp.zeros((1, LANES), F32)
    anyslot = jnp.zeros((peers, LANES), F32)
    for k in range(CAP):
        rank = rank + float(k) * jnp.sum(slots[k], axis=0, keepdims=True)
        anyslot = anyslot + slots[k]
        slot_ref[:, k * LANES : (k + 1) * LANES] = slots[k].astype(BF16)
    rank_ref[...] = jnp.broadcast_to(rank, rank_ref.shape).astype(jnp.int32)
    n = peers * ROWS
    row = iota((n, peers), 0)
    peer = (row * 10923) >> 16
    part = row - peer * ROWS
    same = peer == iota((n, peers), 1)
    main = jnp.zeros((n, LANES), F32)
    for k in range(CAP):
        main = main + dot((same & (part == k)).astype(BF16), slots[k].astype(BF16), ((1,), (0,)))
    tail = dot((same & (part == CAP)).astype(BF16), anyslot.astype(BF16), ((1,), (0,)))
    take_ref[:, :LANES] = main.astype(BF16)
    take_ref[:, LANES:] = tail.astype(BF16)


def mix(ref, f, level, left, here, rows):
    return (
        left * ref[f, level, PAD - 1 : PAD - 1 + rows]
        + here * ref[f, level, PAD : PAD + rows]
        + ref[f, level, PAD + 1 : PAD + 1 + rows]
    )


def put(ref, f, level, x):
    n = x.shape[0]
    ref[f, level, PAD : PAD + n] = x
    ref[f, level, PAD - 1 : PAD] = x[n - 1 :]
    ref[f, level, PAD + n : PAD + n + 1] = x[:1]


def column(levels, mixed, keep):
    def body(level, carry):
        below, here = carry
        above = mixed(jnp.minimum(level + 1, levels - 1))
        keep(level, [8.0 * h + (a + b) for a, h, b in zip(above, here, below, strict=True)])
        return here, above

    start = mixed(0)
    return body, (start, start)


def start_kernel(near_ref, far_ref, left_ref, here_ref, wide_ref, out_ref, load_ref):
    levels = near_ref.shape[1]
    rows = out_ref.shape[2]
    halo = 2 * SUB
    odd = (lax.axis_index("narrow") & 1) == 1

    def add_halo(high_ref, low_ref):
        def load(level, carry):
            sides = [
                jnp.concatenate([high_ref[f, level].astype(F32), low_ref[f, level].astype(F32)], axis=0)
                for f in range(2)
            ]
            sides[0] = sides[0] + 2.0 * sides[1]
            for f in range(2):
                load_ref[f, level, PAD + rows - halo : PAD + rows] = sides[f]
                load_ref[f, level, PAD - 1 : PAD] = sides[f][halo - 1 :]
            return carry

        lax.fori_loop(0, levels, load, 0, unroll=UNROLL)

    @pl.when(odd)
    def _():
        add_halo(far_ref, near_ref)

    @pl.when(jnp.logical_not(odd))
    def _():
        add_halo(near_ref, far_ref)

    def mixed(level):
        left, here = left_ref[pl.ds(level, 1), :], here_ref[pl.ds(level, 1), :]
        return tuple(mix(load_ref, f, level, left, here, rows) for f in range(2))

    def keep(level, pair):
        for f in range(2):
            out_ref[f, level] = pair[f]

    body, carry = column(levels, mixed, keep)
    lax.fori_loop(0, levels, body, carry, unroll=UNROLL)


def main_kernel(
    wire_ref, take_ref, rank_ref, start_ref, crm_ref, left_ref, here_ref, cloud_ref, down_ref,
    new_hbm, diff_ref, force_ref, field_ref, next_ref, new_ref, sems,
):
    levels = crm_ref.shape[1]
    gcm = down_ref.shape[1]
    own = crm_ref.shape[2]
    full = start_ref.shape[2]
    got = dot(wire_ref[...], take_ref[...], ((0,), (0,)))
    tail = jnp.zeros((EXTRA, LANES), F32)
    rank = rank_ref[0:1, :]
    for k in range(CAP):
        tail = tail + jnp.where(rank == k, got[k * EXTRA : (k + 1) * EXTRA, LANES:], 0.0)
    rows = jnp.concatenate([got[:, :LANES], tail], axis=0)
    force = [
        lax.dot_general(
            down_ref[...], rows[f * gcm : (f + 1) * gcm], (((1,), (0,)), ((), ())),
            precision=HI, preferred_element_type=F32,
        )
        for f in range(2)
    ]
    force[0] = force[0] + 2.0 * force[1]
    for index in range(SUB):
        for f in range(2):
            force_ref[index, f, :levels] = (0.25 * STEP ** (index + 1)) * force[f]
    diff_ref[:, levels:] = jnp.zeros((2, diff_ref.shape[1] - levels, LANES), F32)

    def physics(pair, level, index):
        m = pair[0] + force_ref[index, 0, pl.ds(level, 1), :]
        q = pair[1] + force_ref[index, 1, pl.ds(level, 1), :]
        return m, q - cloud_ref[pl.ds(level, 1), :] * jnp.maximum(q, 0.0)

    def first(level, carry):
        pair = physics((start_ref[0, level], start_ref[1, level]), level, 0)
        for f in range(2):
            put(field_ref, f, level, pair[f])
        return carry

    lax.fori_loop(0, levels, first, 0, unroll=UNROLL)
    piece = levels // PIECES
    copies = []
    for index in range(1, SUB):
        last = index == SUB - 1
        source, target = (field_ref, next_ref) if index % 2 else (next_ref, field_ref)
        size = own if last else full

        def mixed(level, source=source, size=size):
            left, here = left_ref[pl.ds(level, 1), :], here_ref[pl.ds(level, 1), :]
            return tuple(mix(source, f, level, left, here, size) for f in range(2))

        def keep(level, pair, index=index, last=last, target=target):
            pair = physics(pair, level, index)
            if not last:
                for f in range(2):
                    put(target, f, level, pair[f])
                return
            scale = STEP**-SUB
            q = scale * pair[1]
            t = scale * pair[0] - 2.0 * q
            for f, x in enumerate((t, q)):
                new_ref[f, level] = x.astype(BF16)
                change = x - crm_ref[f, level].astype(F32)
                diff_ref[f, pl.ds(level, 1), :] = jnp.sum(change, axis=0, keepdims=True)

        body, carry = column(levels, mixed, keep)
        if not last:
            lax.fori_loop(0, levels, body, carry, unroll=UNROLL)
            continue
        for part in range(PIECES):
            carry = lax.fori_loop(part * piece, (part + 1) * piece, body, carry, unroll=UNROLL)
            span = pl.ds(part * piece, piece)
            for f in range(2):
                copy = pltpu.make_async_copy(
                    new_ref.at[f, span], new_hbm.at[f, span], sems.at[2 * part + f]
                )
                copy.start()
                copies.append(copy)
    for copy in copies:
        copy.wait()


def turn_kernel(part_ref, slot_ref, wire_ref):
    total = jnp.sum(part_ref[...], axis=0)
    peers = wire_ref.shape[0]
    rows = total.shape[0]
    wire = jnp.zeros((peers, LANES), F32)
    for piece in split3(total):
        for k in range(CAP):
            padded = []
            if k:
                padded.append(jnp.zeros((k * rows, LANES), F32))
            padded.append(piece.astype(F32))
            if (k + 1) * rows < LANES:
                padded.append(jnp.zeros((LANES - (k + 1) * rows, LANES), F32))
            block = jnp.concatenate(padded, axis=0).astype(BF16)
            wire = wire + dot(slot_ref[:, k * LANES : (k + 1) * LANES], block, ((1,), (1,)))
    wire_ref[...] = wire


def back_kernel(wire_ref, owner_ref, rank_ref, out_ref):
    rows = out_ref.shape[1]
    got = jnp.zeros((LANES, LANES), F32)
    for piece in split3(wire_ref[...]):
        got = got + dot(piece, owner_ref[...], ((0,), (0,)))
    rank = rank_ref[0:1, :]
    change = jnp.zeros((rows, LANES), F32)
    for k in range(CAP):
        change = change + jnp.where(rank == k, got[k * rows : (k + 1) * rows], 0.0)
    out_ref[...] = jnp.broadcast_to(change[None], out_ref.shape)


def sum_kernel(part_ref, out_ref):
    out_ref[...] = jnp.broadcast_to(jnp.sum(part_ref[...], axis=0)[None], out_ref.shape)


def end_kernel(change_ref, up_ref, out_ref):
    levels, gcm = up_ref.shape
    half = change_ref.shape[0] // 2
    for f in range(2):
        tend = lax.dot_general(
            up_ref[...], change_ref[f * half : f * half + levels], (((0,), (0,)), ((), ())),
            precision=HI, preferred_element_type=F32,
        ) * (1.0 / (CX * SUB))
        out_ref[f * gcm : (f + 1) * gcm] = tend.astype(BF16)


VM = pl.BlockSpec(memory_space=pltpu.VMEM)
HB = pl.BlockSpec(memory_space=pltpu.HBM)


def call(kernel, shapes, specs, *args, scratch=(), room=4, outs=None, alias=None):
    out = [jax.ShapeDtypeStruct(s, d) for s, d in shapes]
    many = len(out) > 1
    return pl.pallas_call(
        kernel,
        out_shape=out if many else out[0],
        in_specs=specs,
        out_specs=outs or ([VM] * len(out) if many else VM),
        scratch_shapes=list(scratch),
        input_output_aliases=alias or {},
        compiler_params=pltpu.CompilerParams(vmem_limit_bytes=room << 20),
    )(*args)


def shards(gcm_state, crm_state, courant, cloud_mask, level_down, level_up, column_map):
    peers = lax.axis_size("wide")
    ring = lax.axis_size("narrow")
    columns, width = gcm_state.shape
    levels = crm_state.shape[1]
    own = crm_state.shape[2]
    targets = column_map.reshape(peers, columns)
    n = peers * ROWS
    near = [[g * NEAR + i for i in range(NEAR)] for g in range(ring // NEAR)]
    far = [[g + NEAR * i for i in range(ring // NEAR)] for g in range(NEAR)]
    pairs = [(i, i ^ 1) for i in range(ring)]
    other_pairs = [(i, ((i + 1) ^ 1) - 1) for i in range(ring)]
    other_pairs = [(a, b % ring) for a, b in other_pairs]
    args = (targets, gcm_state.T, crm_state, courant, cloud_mask, level_down, level_up.T)
    resident = [(x.shape, x.dtype) for x in args]

    wire, owner, send_rank, face, other, targets, crm, courant, cloud_mask, down, up = call(
        pack_kernel,
        [((n, LANES), BF16), ((peers, LANES), BF16), ((8, LANES), jnp.int32)]
        + [((2, levels, SUB, LANES), BF16)] * 2
        + resident[:1] + resident[2:],
        [HB] * 7, *[pltpu.with_memory_space_constraint(x, pltpu.HBM) for x in args],
        scratch=[pltpu.VMEM((width, LANES), F32), pltpu.SemaphoreType.DMA((7,))],
    )
    arrived = lax.all_to_all(
        wire.reshape(n // 2, 2, LANES), "wide", split_axis=0, concat_axis=0, tiled=True
    ).reshape(n, LANES)
    halo_far = lax.ppermute(other, "narrow", other_pairs)
    halo_near = lax.ppermute(face, "narrow", pairs)

    full = own + 2 * SUB
    padded = full + 2 * PAD
    slots, take, take_rank, left, here, cloud, widened = call(
        route_kernel,
        [((peers, CAP * LANES), BF16), ((n, 2 * LANES), BF16), ((8, LANES), jnp.int32)]
        + [((levels, LANES), F32)] * 3
        + [((2, levels, padded, LANES), F32)],
        [VM] * 4, targets, crm, courant, cloud_mask,
    )
    started, _ = call(
        start_kernel, [((2, levels, full, LANES), F32), ((2, levels, padded, LANES), F32)],
        [VM] * 5, halo_near, halo_far, left, here, widened,
        room=6, alias={4: 1},
    )
    crm_new, diff = call(
        main_kernel,
        [((2, levels, own, LANES), BF16), ((2, ring * 4, LANES), F32)],
        [VM] * 9,
        arrived, take, take_rank, started, crm, left, here, cloud, down,
        scratch=[
            pltpu.VMEM((SUB, 2, ring * 4, LANES), F32),
            pltpu.VMEM((2, levels, padded, LANES), F32),
            pltpu.VMEM((2, levels, padded, LANES), F32),
            pltpu.VMEM((2, levels, own, LANES), BF16),
            pltpu.SemaphoreType.DMA((2 * PIECES,)),
        ],
        room=12,
        outs=[HB, VM],
    )
    rows = 2 * ring * 4 // NEAR
    parts = lax.all_to_all(
        diff.reshape(NEAR, rows, LANES), "narrow", split_axis=0, concat_axis=0,
        axis_index_groups=near, tiled=True,
    )
    sums = call(sum_kernel, [((NEAR, rows, LANES), F32)], [VM], parts)
    sums = lax.all_to_all(
        sums, "narrow", split_axis=0, concat_axis=0, axis_index_groups=far, tiled=True
    )
    back = call(turn_kernel, [((peers, LANES), F32)], [VM] * 2, sums, slots)
    back = lax.all_to_all(
        back.reshape(peers, 1, LANES), "wide", split_axis=0, concat_axis=0, tiled=True
    ).reshape(peers, LANES)
    change = call(back_kernel, [((NEAR, rows, LANES), F32)], [VM] * 3, back, owner, send_rank)
    change = lax.all_to_all(
        change, "narrow", split_axis=0, concat_axis=0, axis_index_groups=near, tiled=True
    )
    tendency = call(
        end_kernel, [((width, LANES), BF16)], [VM] * 2, change.reshape(NEAR * rows, LANES), up
    )
    return tendency.T, crm_new


def solution(mesh):
    placed = (
        P("wide", None),
        P(None, None, "narrow", "wide"),
        P(None, "wide"),
        P(None, "wide"),
        P(),
        P(),
        P(),
    )

    return jax.shard_map(
        shards,
        mesh=mesh,
        in_specs=placed,
        out_specs=(P("wide", None), P(None, None, "narrow", "wide")),
        check_vma=False,
    )
```

```python
import jax
import jax.numpy as jnp
from jax import lax
from jax.experimental import pallas as pl
from jax.experimental.pallas import tpu as pltpu
from jax.sharding import PartitionSpec as P


CX = 256
SUB = 4
CAP = 4
ROWS = 6
LANES = 128
EXTRA = 16
NEAR = 4
HEAD = 36
SIDE = 0.15
STEP = 1.0 / (0.1 * SIDE)
PAD = 8
PIECES = 3
UNROLL = 5
HI = lax.Precision.HIGHEST
F32 = jnp.float32
BF16 = jnp.bfloat16


def iota(shape, dim):
    return lax.broadcasted_iota(jnp.int32, shape, dim)


def dot(a, b, dims):
    return lax.dot_general(a, b, (dims, ((), ())), preferred_element_type=F32)


def split3(x):
    a = x.astype(BF16)
    r = x - a.astype(F32)
    b = r.astype(BF16)
    c = (r - b.astype(F32)).astype(BF16)
    return a, b, c


def row_parts(start):
    row = iota((LANES, LANES), 0) + start
    peer = (row * 10923) >> 16
    return peer ^ HEAD, row - peer * ROWS


def before_matrix():
    return (iota((LANES, LANES), 0) < iota((LANES, LANES), 1)).astype(BF16)


def pack_kernel(
    map_hbm, state_hbm, crm_hbm, courant_hbm, mask_hbm, down_hbm, up_hbm,
    wire_ref, owner_ref, rank_ref, face_ref, other_ref,
    map_ref, crm_ref, courant_ref, mask_ref, down_ref, up_ref,
    state_ref, sems,
):
    pairs = (
        (map_hbm, map_ref), (state_hbm, state_ref), (crm_hbm, crm_ref), (courant_hbm, courant_ref),
        (mask_hbm, mask_ref), (down_hbm, down_ref), (up_hbm, up_ref),
    )
    copies = [pltpu.make_async_copy(a, b, sems.at[i]) for i, (a, b) in enumerate(pairs)]
    for copy in copies:
        copy.start()
    copies[0].wait()
    peers = map_ref.shape[0]
    mine = map_ref[pl.ds(lax.axis_index("wide"), 1), :] >> 7
    own = (iota((peers, LANES), 0) ^ HEAD) == mine
    own_b = own.astype(BF16)
    count = dot(own_b, before_matrix(), ((1,), (0,)))
    rank = jnp.sum(jnp.where(own, count, 0.0), axis=0, keepdims=True).astype(jnp.int32)
    owner_ref[...] = own_b
    rank_ref[...] = jnp.broadcast_to(rank, rank_ref.shape)
    copies[1].wait()
    state = state_ref[...].astype(BF16)
    levels = state.shape[0]
    extra = state[LANES:levels].astype(F32)
    spread = [jnp.where(rank == k, extra, 0.0) for k in range(CAP)]
    spread.append(jnp.zeros((LANES - CAP * EXTRA, LANES), F32))
    spread = jnp.concatenate(spread, axis=0).astype(BF16)
    for start in range(0, peers * ROWS, LANES):
        peer, part = row_parts(start)
        to_peer = peer == mine
        main = (to_peer & (part == rank)).astype(BF16)
        tail = (to_peer & (part == CAP)).astype(BF16)
        wire = dot(main, state[:LANES], ((1,), (1,))) + dot(tail, spread, ((1,), (1,)))
        wire_ref[start : start + LANES] = wire.astype(BF16)
    copies[2].wait()
    own_columns = crm_ref.shape[2]
    odd = (lax.axis_index("narrow") & 1) == 1

    def faces(to_low, to_high):
        def body(level, carry):
            for f in range(2):
                to_low[f, level] = crm_ref[f, level, :SUB]
                to_high[f, level] = crm_ref[f, level, own_columns - SUB :]
            return carry

        lax.fori_loop(0, crm_ref.shape[1], body, 0, unroll=UNROLL)

    @pl.when(odd)
    def _():
        faces(face_ref, other_ref)

    @pl.when(jnp.logical_not(odd))
    def _():
        faces(other_ref, face_ref)

    for copy in copies[3:]:
        copy.wait()


def route_kernel(
    map_ref, crm_ref, courant_ref, mask_ref,
    slot_ref, take_ref, rank_ref, left_ref, here_ref, cloud_ref, wide_ref,
):
    own = crm_ref.shape[2]

    def widen(level, carry):
        q = crm_ref[1, level].astype(F32)
        m = crm_ref[0, level].astype(F32) + 2.0 * q
        for f, x in enumerate((m, q)):
            wide_ref[f, level, PAD : PAD + own] = x
            wide_ref[f, level, PAD + own + 2 * SUB : PAD + own + 2 * SUB + 1] = x[:1]
        return carry

    lax.fori_loop(0, crm_ref.shape[1], widen, 0, unroll=UNROLL)
    left_ref[...] = courant_ref[...] * (1.0 / SIDE) + 1.0
    here_ref[...] = (0.7 - courant_ref[...]) * (1.0 / SIDE)
    cloud_ref[...] = mask_ref[...].astype(F32) * 0.3
    peers = map_ref.shape[0]
    targets = map_ref[...]
    here = (targets >> 7) == lax.axis_index("wide")
    local = (targets & (LANES - 1)).astype(F32) + 1.0
    count = dot(here.astype(BF16), before_matrix(), ((1,), (0,)))
    slots = []
    lane = iota((peers, LANES), 1).astype(F32) + 1.0
    for k in range(CAP):
        hit = here & (count == float(k))
        one = jnp.sum(jnp.where(hit, local, 0.0), axis=1, keepdims=True)
        slots.append((one == lane).astype(F32))
    swap = ((iota((peers, peers), 0) ^ HEAD) == iota((peers, peers), 1)).astype(BF16)
    rank = jnp.zeros((1, LANES), F32)
    anyslot = jnp.zeros((peers, LANES), F32)
    for k in range(CAP):
        rank = rank + float(k) * jnp.sum(slots[k], axis=0, keepdims=True)
        anyslot = anyslot + slots[k]
        moved = dot(swap, slots[k].astype(BF16), ((1,), (0,)))
        slot_ref[:, k * LANES : (k + 1) * LANES] = moved.astype(BF16)
    rank_ref[...] = jnp.broadcast_to(rank, rank_ref.shape).astype(jnp.int32)
    n = peers * ROWS
    row = iota((n, peers), 0)
    peer = (row * 10923) >> 16
    part = row - peer * ROWS
    same = (peer ^ HEAD) == iota((n, peers), 1)
    main = jnp.zeros((n, LANES), F32)
    for k in range(CAP):
        main = main + dot((same & (part == k)).astype(BF16), slots[k].astype(BF16), ((1,), (0,)))
    tail = dot((same & (part == CAP)).astype(BF16), anyslot.astype(BF16), ((1,), (0,)))
    take_ref[:, :LANES] = main.astype(BF16)
    take_ref[:, LANES:] = tail.astype(BF16)


def mix(ref, f, level, left, here, rows):
    return (
        left * ref[f, level, PAD - 1 : PAD - 1 + rows]
        + here * ref[f, level, PAD : PAD + rows]
        + ref[f, level, PAD + 1 : PAD + 1 + rows]
    )


def put(ref, f, level, x):
    n = x.shape[0]
    ref[f, level, PAD : PAD + n] = x
    ref[f, level, PAD - 1 : PAD] = x[n - 1 :]
    ref[f, level, PAD + n : PAD + n + 1] = x[:1]


def column(levels, mixed, keep):
    def body(level, carry):
        below, here = carry
        above = mixed(jnp.minimum(level + 1, levels - 1))
        keep(level, [8.0 * h + (a + b) for a, h, b in zip(above, here, below, strict=True)])
        return here, above

    start = mixed(0)
    return body, (start, start)


def start_kernel(near_ref, far_ref, left_ref, here_ref, wide_ref, out_ref, load_ref):
    levels = near_ref.shape[1]
    rows = out_ref.shape[2]
    halo = 2 * SUB
    odd = (lax.axis_index("narrow") & 1) == 1

    def add_halo(high_ref, low_ref):
        def load(level, carry):
            sides = [
                jnp.concatenate([high_ref[f, level].astype(F32), low_ref[f, level].astype(F32)], axis=0)
                for f in range(2)
            ]
            sides[0] = sides[0] + 2.0 * sides[1]
            for f in range(2):
                load_ref[f, level, PAD + rows - halo : PAD + rows] = sides[f]
                load_ref[f, level, PAD - 1 : PAD] = sides[f][halo - 1 :]
            return carry

        lax.fori_loop(0, levels, load, 0, unroll=UNROLL)

    @pl.when(odd)
    def _():
        add_halo(far_ref, near_ref)

    @pl.when(jnp.logical_not(odd))
    def _():
        add_halo(near_ref, far_ref)

    def mixed(level):
        left, here = left_ref[pl.ds(level, 1), :], here_ref[pl.ds(level, 1), :]
        return tuple(mix(load_ref, f, level, left, here, rows) for f in range(2))

    def keep(level, pair):
        for f in range(2):
            out_ref[f, level] = pair[f]

    body, carry = column(levels, mixed, keep)
    lax.fori_loop(0, levels, body, carry, unroll=UNROLL)


def main_kernel(
    wire_ref, take_ref, rank_ref, start_ref, crm_ref, left_ref, here_ref, cloud_ref, down_ref,
    new_hbm, diff_ref, force_ref, field_ref, next_ref, new_ref, sems,
):
    levels = crm_ref.shape[1]
    gcm = down_ref.shape[1]
    own = crm_ref.shape[2]
    full = start_ref.shape[2]
    got = dot(wire_ref[...], take_ref[...], ((0,), (0,)))
    tail = jnp.zeros((EXTRA, LANES), F32)
    rank = rank_ref[0:1, :]
    for k in range(CAP):
        tail = tail + jnp.where(rank == k, got[k * EXTRA : (k + 1) * EXTRA, LANES:], 0.0)
    rows = jnp.concatenate([got[:, :LANES], tail], axis=0)
    force = [
        lax.dot_general(
            down_ref[...], rows[f * gcm : (f + 1) * gcm], (((1,), (0,)), ((), ())),
            precision=HI, preferred_element_type=F32,
        )
        for f in range(2)
    ]
    force[0] = force[0] + 2.0 * force[1]
    for index in range(SUB):
        for f in range(2):
            force_ref[index, f, :levels] = (0.25 * STEP ** (index + 1)) * force[f]
    diff_ref[:, levels:] = jnp.zeros((2, diff_ref.shape[1] - levels, LANES), F32)

    def physics(pair, level, index):
        m = pair[0] + force_ref[index, 0, pl.ds(level, 1), :]
        q = pair[1] + force_ref[index, 1, pl.ds(level, 1), :]
        return m, q - cloud_ref[pl.ds(level, 1), :] * jnp.maximum(q, 0.0)

    def first(level, carry):
        pair = physics((start_ref[0, level], start_ref[1, level]), level, 0)
        for f in range(2):
            put(field_ref, f, level, pair[f])
        return carry

    lax.fori_loop(0, levels, first, 0, unroll=UNROLL)
    piece = levels // PIECES
    copies = []
    for index in range(1, SUB):
        last = index == SUB - 1
        source, target = (field_ref, next_ref) if index % 2 else (next_ref, field_ref)
        size = own if last else full

        def mixed(level, source=source, size=size):
            left, here = left_ref[pl.ds(level, 1), :], here_ref[pl.ds(level, 1), :]
            return tuple(mix(source, f, level, left, here, size) for f in range(2))

        def keep(level, pair, index=index, last=last, target=target):
            pair = physics(pair, level, index)
            if not last:
                for f in range(2):
                    put(target, f, level, pair[f])
                return
            scale = STEP**-SUB
            q = scale * pair[1]
            t = scale * pair[0] - 2.0 * q
            for f, x in enumerate((t, q)):
                new_ref[f, level] = x.astype(BF16)
                change = x - crm_ref[f, level].astype(F32)
                diff_ref[f, pl.ds(level, 1), :] = jnp.sum(change, axis=0, keepdims=True)

        body, carry = column(levels, mixed, keep)
        if not last:
            lax.fori_loop(0, levels, body, carry, unroll=UNROLL)
            continue
        for part in range(PIECES):
            carry = lax.fori_loop(part * piece, (part + 1) * piece, body, carry, unroll=UNROLL)
            span = pl.ds(part * piece, piece)
            for f in range(2):
                copy = pltpu.make_async_copy(
                    new_ref.at[f, span], new_hbm.at[f, span], sems.at[2 * part + f]
                )
                copy.start()
                copies.append(copy)
    for copy in copies:
        copy.wait()


def turn_kernel(part_ref, slot_ref, wire_ref):
    total = jnp.sum(part_ref[...], axis=0)
    peers = wire_ref.shape[0]
    rows = total.shape[0]
    wire = jnp.zeros((peers, LANES), F32)
    for piece in split3(total):
        for k in range(CAP):
            padded = []
            if k:
                padded.append(jnp.zeros((k * rows, LANES), F32))
            padded.append(piece.astype(F32))
            if (k + 1) * rows < LANES:
                padded.append(jnp.zeros((LANES - (k + 1) * rows, LANES), F32))
            block = jnp.concatenate(padded, axis=0).astype(BF16)
            wire = wire + dot(slot_ref[:, k * LANES : (k + 1) * LANES], block, ((1,), (1,)))
    wire_ref[...] = wire


def back_kernel(wire_ref, owner_ref, rank_ref, out_ref):
    rows = out_ref.shape[1]
    got = jnp.zeros((LANES, LANES), F32)
    for piece in split3(wire_ref[...]):
        got = got + dot(piece, owner_ref[...], ((0,), (0,)))
    rank = rank_ref[0:1, :]
    change = jnp.zeros((rows, LANES), F32)
    for k in range(CAP):
        change = change + jnp.where(rank == k, got[k * rows : (k + 1) * rows], 0.0)
    out_ref[...] = jnp.broadcast_to(change[None], out_ref.shape)


def sum_kernel(part_ref, out_ref):
    out_ref[...] = jnp.broadcast_to(jnp.sum(part_ref[...], axis=0)[None], out_ref.shape)


def end_kernel(change_ref, up_ref, out_ref):
    levels, gcm = up_ref.shape
    half = change_ref.shape[0] // 2
    for f in range(2):
        tend = lax.dot_general(
            up_ref[...], change_ref[f * half : f * half + levels], (((0,), (0,)), ((), ())),
            precision=HI, preferred_element_type=F32,
        ) * (1.0 / (CX * SUB))
        out_ref[f * gcm : (f + 1) * gcm] = tend.astype(BF16)


VM = pl.BlockSpec(memory_space=pltpu.VMEM)
HB = pl.BlockSpec(memory_space=pltpu.HBM)


def call(kernel, shapes, specs, *args, scratch=(), room=4, outs=None, alias=None):
    out = [jax.ShapeDtypeStruct(s, d) for s, d in shapes]
    many = len(out) > 1
    return pl.pallas_call(
        kernel,
        out_shape=out if many else out[0],
        in_specs=specs,
        out_specs=outs or ([VM] * len(out) if many else VM),
        scratch_shapes=list(scratch),
        input_output_aliases=alias or {},
        compiler_params=pltpu.CompilerParams(vmem_limit_bytes=room << 20),
    )(*args)


def shards(gcm_state, crm_state, courant, cloud_mask, level_down, level_up, column_map):
    peers = lax.axis_size("wide")
    ring = lax.axis_size("narrow")
    columns, width = gcm_state.shape
    levels = crm_state.shape[1]
    own = crm_state.shape[2]
    targets = column_map.reshape(peers, columns)
    n = peers * ROWS
    wide = [[p ^ HEAD for p in range(peers)]]
    near = [[g * NEAR + i for i in reversed(range(NEAR))] for g in range(ring // NEAR)]
    far = [[g + NEAR * i for i in (2, 3, 1, 0)] for g in range(NEAR)]
    pairs = [(i, i ^ 1) for i in range(ring)]
    other_pairs = [(i, ((i + 1) ^ 1) - 1) for i in range(ring)]
    other_pairs = [(a, b % ring) for a, b in other_pairs]
    args = (targets, gcm_state.T, crm_state, courant, cloud_mask, level_down, level_up.T)
    resident = [(x.shape, x.dtype) for x in args]

    wire, owner, send_rank, face, other, targets, crm, courant, cloud_mask, down, up = call(
        pack_kernel,
        [((n, LANES), BF16), ((peers, LANES), BF16), ((8, LANES), jnp.int32)]
        + [((2, levels, SUB, LANES), BF16)] * 2
        + resident[:1] + resident[2:],
        [HB] * 7, *[pltpu.with_memory_space_constraint(x, pltpu.HBM) for x in args],
        scratch=[pltpu.VMEM((width, LANES), F32), pltpu.SemaphoreType.DMA((7,))],
    )
    arrived = lax.all_to_all(
        wire.reshape(n // 2, 2, LANES), "wide", split_axis=0, concat_axis=0,
        axis_index_groups=wide, tiled=True,
    ).reshape(n, LANES)
    halo_far = lax.ppermute(other, "narrow", other_pairs)
    halo_near = lax.ppermute(face, "narrow", pairs)

    full = own + 2 * SUB
    padded = full + 2 * PAD
    slots, take, take_rank, left, here, cloud, widened = call(
        route_kernel,
        [((peers, CAP * LANES), BF16), ((n, 2 * LANES), BF16), ((8, LANES), jnp.int32)]
        + [((levels, LANES), F32)] * 3
        + [((2, levels, padded, LANES), F32)],
        [VM] * 4, targets, crm, courant, cloud_mask,
    )
    started, _ = call(
        start_kernel, [((2, levels, full, LANES), F32), ((2, levels, padded, LANES), F32)],
        [VM] * 5, halo_near, halo_far, left, here, widened,
        room=6, alias={4: 1},
    )
    crm_new, diff = call(
        main_kernel,
        [((2, levels, own, LANES), BF16), ((2, ring * 4, LANES), F32)],
        [VM] * 9,
        arrived, take, take_rank, started, crm, left, here, cloud, down,
        scratch=[
            pltpu.VMEM((SUB, 2, ring * 4, LANES), F32),
            pltpu.VMEM((2, levels, padded, LANES), F32),
            pltpu.VMEM((2, levels, padded, LANES), F32),
            pltpu.VMEM((2, levels, own, LANES), BF16),
            pltpu.SemaphoreType.DMA((2 * PIECES,)),
        ],
        room=12,
        outs=[HB, VM],
    )
    rows = 2 * ring * 4 // NEAR
    parts = lax.all_to_all(
        diff.reshape(NEAR, rows, LANES), "narrow", split_axis=0, concat_axis=0,
        axis_index_groups=near, tiled=True,
    )
    sums = call(sum_kernel, [((NEAR, rows, LANES), F32)], [VM], parts)
    sums = lax.all_to_all(
        sums, "narrow", split_axis=0, concat_axis=0, axis_index_groups=far, tiled=True
    )
    back = call(turn_kernel, [((peers, LANES), F32)], [VM] * 2, sums, slots)
    back = lax.all_to_all(
        back.reshape(peers, 1, LANES), "wide", split_axis=0, concat_axis=0,
        axis_index_groups=wide, tiled=True,
    ).reshape(peers, LANES)
    change = call(back_kernel, [((NEAR, rows, LANES), F32)], [VM] * 3, back, owner, send_rank)
    change = lax.all_to_all(
        change, "narrow", split_axis=0, concat_axis=0, axis_index_groups=near, tiled=True
    )
    tendency = call(
        end_kernel, [((width, LANES), BF16)], [VM] * 2, change.reshape(NEAR * rows, LANES), up
    )
    return tendency.T, crm_new


def solution(mesh):
    placed = (
        P("wide", None),
        P(None, None, "narrow", "wide"),
        P(None, "wide"),
        P(None, "wide"),
        P(),
        P(),
        P(),
    )

    return jax.shard_map(
        shards,
        mesh=mesh,
        in_specs=placed,
        out_specs=(P("wide", None), P(None, None, "narrow", "wide")),
        check_vma=False,
    )
```

```python
import jax
import jax.numpy as jnp
from jax import lax
from jax.experimental import pallas as pl
from jax.experimental.pallas import tpu as pltpu
from jax.sharding import PartitionSpec as P


CX = 256
SUB = 4
CAP = 4
ROWS = 6
LANES = 128
EXTRA = 16
NEAR = 4
HEAD = 36
SIDE = 0.15
STEP = 1.0 / (0.1 * SIDE)
PAD = 8
PIECES = 3
UNROLL = 5
HI = lax.Precision.HIGHEST
F32 = jnp.float32
BF16 = jnp.bfloat16


def iota(shape, dim):
    return lax.broadcasted_iota(jnp.int32, shape, dim)


def dot(a, b, dims):
    return lax.dot_general(a, b, (dims, ((), ())), preferred_element_type=F32)


def split3(x):
    a = x.astype(BF16)
    r = x - a.astype(F32)
    b = r.astype(BF16)
    c = (r - b.astype(F32)).astype(BF16)
    return a, b, c


def row_parts(start):
    row = iota((LANES, LANES), 0) + start
    peer = (row * 10923) >> 16
    return peer ^ HEAD, row - peer * ROWS


def before_matrix():
    return (iota((LANES, LANES), 0) < iota((LANES, LANES), 1)).astype(BF16)


def pack_kernel(
    map_hbm, state_hbm, crm_hbm, courant_hbm, mask_hbm, down_hbm, up_hbm,
    wire_hbm, owner_ref, rank_ref, face_ref, other_ref,
    map_ref, crm_ref, courant_ref, mask_ref, down_ref, up_ref,
    state_ref, wire_ref, sems, out_sems,
):
    pairs = (
        (map_hbm, map_ref), (state_hbm, state_ref), (crm_hbm, crm_ref), (courant_hbm, courant_ref),
        (mask_hbm, mask_ref), (down_hbm, down_ref), (up_hbm, up_ref),
    )
    copies = [pltpu.make_async_copy(a, b, sems.at[i]) for i, (a, b) in enumerate(pairs)]
    for copy in copies:
        copy.start()
    copies[0].wait()
    peers = map_ref.shape[0]
    mine = map_ref[pl.ds(lax.axis_index("wide"), 1), :] >> 7
    own = (iota((peers, LANES), 0) ^ HEAD) == mine
    own_b = own.astype(BF16)
    count = dot(own_b, before_matrix(), ((1,), (0,)))
    rank = jnp.sum(jnp.where(own, count, 0.0), axis=0, keepdims=True).astype(jnp.int32)
    owner_ref[...] = own_b
    rank_ref[...] = jnp.broadcast_to(rank, rank_ref.shape)
    copies[1].wait()
    state = state_ref[...].astype(BF16)
    levels = state.shape[0]
    extra = state[LANES:levels].astype(F32)
    spread = [jnp.where(rank == k, extra, 0.0) for k in range(CAP)]
    spread.append(jnp.zeros((LANES - CAP * EXTRA, LANES), F32))
    spread = jnp.concatenate(spread, axis=0).astype(BF16)
    for start in range(0, peers * ROWS, LANES):
        peer, part = row_parts(start)
        to_peer = peer == mine
        main = (to_peer & (part == rank)).astype(BF16)
        tail = (to_peer & (part == CAP)).astype(BF16)
        wire = dot(main, state[:LANES], ((1,), (1,))) + dot(tail, spread, ((1,), (1,)))
        rows = pl.ds(start, LANES)
        wire_ref[rows] = wire.astype(BF16)
        out = pltpu.make_async_copy(
            wire_ref.at[rows], wire_hbm.at[rows], out_sems.at[start // LANES]
        )
        out.start()
        copies.append(out)
    copies[2].wait()
    own_columns = crm_ref.shape[2]
    odd = (lax.axis_index("narrow") & 1) == 1

    def faces(to_low, to_high):
        def body(level, carry):
            for f in range(2):
                to_low[f, level] = crm_ref[f, level, :SUB]
                to_high[f, level] = crm_ref[f, level, own_columns - SUB :]
            return carry

        lax.fori_loop(0, crm_ref.shape[1], body, 0, unroll=UNROLL)

    @pl.when(odd)
    def _():
        faces(face_ref, other_ref)

    @pl.when(jnp.logical_not(odd))
    def _():
        faces(other_ref, face_ref)

    for copy in copies[3:]:
        copy.wait()


def route_kernel(
    map_ref, crm_ref, courant_ref, mask_ref,
    slot_ref, take_ref, rank_ref, left_ref, here_ref, cloud_ref, wide_ref,
):
    own = crm_ref.shape[2]

    def widen(level, carry):
        q = crm_ref[1, level].astype(F32)
        m = crm_ref[0, level].astype(F32) + 2.0 * q
        for f, x in enumerate((m, q)):
            wide_ref[f, level, PAD : PAD + own] = x
            wide_ref[f, level, PAD + own + 2 * SUB : PAD + own + 2 * SUB + 1] = x[:1]
        return carry

    lax.fori_loop(0, crm_ref.shape[1], widen, 0, unroll=UNROLL)
    left_ref[...] = courant_ref[...] * (1.0 / SIDE) + 1.0
    here_ref[...] = (0.7 - courant_ref[...]) * (1.0 / SIDE)
    cloud_ref[...] = mask_ref[...].astype(F32) * 0.3
    peers = map_ref.shape[0]
    targets = map_ref[...]
    here = (targets >> 7) == lax.axis_index("wide")
    local = (targets & (LANES - 1)).astype(F32) + 1.0
    count = dot(here.astype(BF16), before_matrix(), ((1,), (0,)))
    slots = []
    lane = iota((peers, LANES), 1).astype(F32) + 1.0
    for k in range(CAP):
        hit = here & (count == float(k))
        one = jnp.sum(jnp.where(hit, local, 0.0), axis=1, keepdims=True)
        slots.append((one == lane).astype(F32))
    swap = ((iota((peers, peers), 0) ^ HEAD) == iota((peers, peers), 1)).astype(BF16)
    rank = jnp.zeros((1, LANES), F32)
    anyslot = jnp.zeros((peers, LANES), F32)
    for k in range(CAP):
        rank = rank + float(k) * jnp.sum(slots[k], axis=0, keepdims=True)
        anyslot = anyslot + slots[k]
        moved = dot(swap, slots[k].astype(BF16), ((1,), (0,)))
        slot_ref[:, k * LANES : (k + 1) * LANES] = moved.astype(BF16)
    rank_ref[...] = jnp.broadcast_to(rank, rank_ref.shape).astype(jnp.int32)
    n = peers * ROWS
    row = iota((n, peers), 0)
    peer = (row * 10923) >> 16
    part = row - peer * ROWS
    same = (peer ^ HEAD) == iota((n, peers), 1)
    main = jnp.zeros((n, LANES), F32)
    for k in range(CAP):
        main = main + dot((same & (part == k)).astype(BF16), slots[k].astype(BF16), ((1,), (0,)))
    tail = dot((same & (part == CAP)).astype(BF16), anyslot.astype(BF16), ((1,), (0,)))
    take_ref[:, :LANES] = main.astype(BF16)
    take_ref[:, LANES:] = tail.astype(BF16)


def mix(ref, f, level, left, here, rows):
    return (
        left * ref[f, level, PAD - 1 : PAD - 1 + rows]
        + here * ref[f, level, PAD : PAD + rows]
        + ref[f, level, PAD + 1 : PAD + 1 + rows]
    )


def put(ref, f, level, x):
    n = x.shape[0]
    ref[f, level, PAD : PAD + n] = x
    ref[f, level, PAD - 1 : PAD] = x[n - 1 :]
    ref[f, level, PAD + n : PAD + n + 1] = x[:1]


def column(levels, mixed, keep):
    def body(level, carry):
        below, here = carry
        above = mixed(jnp.minimum(level + 1, levels - 1))
        keep(level, [8.0 * h + (a + b) for a, h, b in zip(above, here, below, strict=True)])
        return here, above

    start = mixed(0)
    return body, (start, start)


def start_kernel(near_ref, far_ref, left_ref, here_ref, wide_ref, out_ref, load_ref):
    levels = near_ref.shape[1]
    rows = out_ref.shape[2]
    halo = 2 * SUB
    odd = (lax.axis_index("narrow") & 1) == 1

    def add_halo(high_ref, low_ref):
        def load(level, carry):
            sides = [
                jnp.concatenate([high_ref[f, level].astype(F32), low_ref[f, level].astype(F32)], axis=0)
                for f in range(2)
            ]
            sides[0] = sides[0] + 2.0 * sides[1]
            for f in range(2):
                load_ref[f, level, PAD + rows - halo : PAD + rows] = sides[f]
                load_ref[f, level, PAD - 1 : PAD] = sides[f][halo - 1 :]
            return carry

        lax.fori_loop(0, levels, load, 0, unroll=UNROLL)

    @pl.when(odd)
    def _():
        add_halo(far_ref, near_ref)

    @pl.when(jnp.logical_not(odd))
    def _():
        add_halo(near_ref, far_ref)

    def mixed(level):
        left, here = left_ref[pl.ds(level, 1), :], here_ref[pl.ds(level, 1), :]
        return tuple(mix(load_ref, f, level, left, here, rows) for f in range(2))

    def keep(level, pair):
        for f in range(2):
            out_ref[f, level] = pair[f]

    body, carry = column(levels, mixed, keep)
    lax.fori_loop(0, levels, body, carry, unroll=UNROLL)


def main_kernel(
    wire_ref, take_ref, rank_ref, start_ref, crm_ref, left_ref, here_ref, cloud_ref, down_ref,
    new_hbm, diff_ref, force_ref, field_ref, next_ref, new_ref, sems,
):
    levels = crm_ref.shape[1]
    gcm = down_ref.shape[1]
    own = crm_ref.shape[2]
    full = start_ref.shape[2]
    got = dot(wire_ref[...], take_ref[...], ((0,), (0,)))
    tail = jnp.zeros((EXTRA, LANES), F32)
    rank = rank_ref[0:1, :]
    for k in range(CAP):
        tail = tail + jnp.where(rank == k, got[k * EXTRA : (k + 1) * EXTRA, LANES:], 0.0)
    rows = jnp.concatenate([got[:, :LANES], tail], axis=0)
    force = [
        lax.dot_general(
            down_ref[...], rows[f * gcm : (f + 1) * gcm], (((1,), (0,)), ((), ())),
            precision=HI, preferred_element_type=F32,
        )
        for f in range(2)
    ]
    force[0] = force[0] + 2.0 * force[1]
    for index in range(SUB):
        for f in range(2):
            force_ref[index, f, :levels] = (0.25 * STEP ** (index + 1)) * force[f]
    diff_ref[:, levels:] = jnp.zeros((2, diff_ref.shape[1] - levels, LANES), F32)

    def physics(pair, level, index):
        m = pair[0] + force_ref[index, 0, pl.ds(level, 1), :]
        q = pair[1] + force_ref[index, 1, pl.ds(level, 1), :]
        return m, q - cloud_ref[pl.ds(level, 1), :] * jnp.maximum(q, 0.0)

    def first(level, carry):
        pair = physics((start_ref[0, level], start_ref[1, level]), level, 0)
        for f in range(2):
            put(field_ref, f, level, pair[f])
        return carry

    lax.fori_loop(0, levels, first, 0, unroll=UNROLL)
    piece = levels // PIECES
    copies = []
    for index in range(1, SUB):
        last = index == SUB - 1
        source, target = (field_ref, next_ref) if index % 2 else (next_ref, field_ref)
        size = own if last else full

        def mixed(level, source=source, size=size):
            left, here = left_ref[pl.ds(level, 1), :], here_ref[pl.ds(level, 1), :]
            return tuple(mix(source, f, level, left, here, size) for f in range(2))

        def keep(level, pair, index=index, last=last, target=target):
            pair = physics(pair, level, index)
            if not last:
                for f in range(2):
                    put(target, f, level, pair[f])
                return
            scale = STEP**-SUB
            q = scale * pair[1]
            t = scale * pair[0] - 2.0 * q
            for f, x in enumerate((t, q)):
                new_ref[f, level] = x.astype(BF16)
                change = x - crm_ref[f, level].astype(F32)
                diff_ref[f, pl.ds(level, 1), :] = jnp.sum(change, axis=0, keepdims=True)

        body, carry = column(levels, mixed, keep)
        if not last:
            lax.fori_loop(0, levels, body, carry, unroll=UNROLL)
            continue
        for part in range(PIECES):
            carry = lax.fori_loop(part * piece, (part + 1) * piece, body, carry, unroll=UNROLL)
            span = pl.ds(part * piece, piece)
            for f in range(2):
                copy = pltpu.make_async_copy(
                    new_ref.at[f, span], new_hbm.at[f, span], sems.at[2 * part + f]
                )
                copy.start()
                copies.append(copy)
    for copy in copies:
        copy.wait()


def turn_kernel(part_ref, slot_ref, wire_ref):
    total = jnp.sum(part_ref[...], axis=0)
    peers = wire_ref.shape[0]
    rows = total.shape[0]
    wire = jnp.zeros((peers, LANES), F32)
    for piece in split3(total):
        for k in range(CAP):
            padded = []
            if k:
                padded.append(jnp.zeros((k * rows, LANES), F32))
            padded.append(piece.astype(F32))
            if (k + 1) * rows < LANES:
                padded.append(jnp.zeros((LANES - (k + 1) * rows, LANES), F32))
            block = jnp.concatenate(padded, axis=0).astype(BF16)
            wire = wire + dot(slot_ref[:, k * LANES : (k + 1) * LANES], block, ((1,), (1,)))
    wire_ref[...] = wire


def back_kernel(wire_ref, owner_ref, rank_ref, out_ref):
    rows = out_ref.shape[1]
    got = jnp.zeros((LANES, LANES), F32)
    for piece in split3(wire_ref[...]):
        got = got + dot(piece, owner_ref[...], ((0,), (0,)))
    rank = rank_ref[0:1, :]
    change = jnp.zeros((rows, LANES), F32)
    for k in range(CAP):
        change = change + jnp.where(rank == k, got[k * rows : (k + 1) * rows], 0.0)
    out_ref[...] = jnp.broadcast_to(change[None], out_ref.shape)


def sum_kernel(part_ref, out_ref):
    out_ref[...] = jnp.broadcast_to(jnp.sum(part_ref[...], axis=0)[None], out_ref.shape)


def end_kernel(change_ref, up_ref, out_hbm, out_ref, sems):
    levels, gcm = up_ref.shape
    half = change_ref.shape[0] // 2
    copies = []
    for f in range(2):
        tend = lax.dot_general(
            up_ref[...], change_ref[f * half : f * half + levels], (((0,), (0,)), ((), ())),
            precision=HI, preferred_element_type=F32,
        ) * (1.0 / (CX * SUB))
        rows = pl.ds(f * gcm, gcm)
        out_ref[f] = tend.astype(BF16)
        copy = pltpu.make_async_copy(out_ref.at[f], out_hbm.at[rows], sems.at[f])
        copy.start()
        copies.append(copy)
    for copy in copies:
        copy.wait()


VM = pl.BlockSpec(memory_space=pltpu.VMEM)
HB = pl.BlockSpec(memory_space=pltpu.HBM)


def call(kernel, shapes, specs, *args, scratch=(), room=4, outs=None, alias=None):
    out = [jax.ShapeDtypeStruct(s, d) for s, d in shapes]
    many = len(out) > 1
    return pl.pallas_call(
        kernel,
        out_shape=out if many else out[0],
        in_specs=specs,
        out_specs=outs or ([VM] * len(out) if many else VM),
        scratch_shapes=list(scratch),
        input_output_aliases=alias or {},
        compiler_params=pltpu.CompilerParams(vmem_limit_bytes=room << 20),
    )(*args)


def shards(gcm_state, crm_state, courant, cloud_mask, level_down, level_up, column_map):
    peers = lax.axis_size("wide")
    ring = lax.axis_size("narrow")
    columns, width = gcm_state.shape
    levels = crm_state.shape[1]
    own = crm_state.shape[2]
    targets = column_map.reshape(peers, columns)
    n = peers * ROWS
    wide = [[p ^ HEAD for p in range(peers)]]
    near = [[g * NEAR + i for i in reversed(range(NEAR))] for g in range(ring // NEAR)]
    far = [[g + NEAR * i for i in (2, 3, 1, 0)] for g in range(NEAR)]
    pairs = [(i, i ^ 1) for i in range(ring)]
    other_pairs = [(i, ((i + 1) ^ 1) - 1) for i in range(ring)]
    other_pairs = [(a, b % ring) for a, b in other_pairs]
    args = (targets, gcm_state.T, crm_state, courant, cloud_mask, level_down, level_up.T)
    resident = [(x.shape, x.dtype) for x in args]

    wire, owner, send_rank, face, other, targets, crm, courant, cloud_mask, down, up = call(
        pack_kernel,
        [((n, LANES), BF16), ((peers, LANES), BF16), ((8, LANES), jnp.int32)]
        + [((2, levels, SUB, LANES), BF16)] * 2
        + resident[:1] + resident[2:],
        [HB] * 7, *[pltpu.with_memory_space_constraint(x, pltpu.HBM) for x in args],
        scratch=[
            pltpu.VMEM((width, LANES), F32),
            pltpu.VMEM((n, LANES), BF16),
            pltpu.SemaphoreType.DMA((7,)),
            pltpu.SemaphoreType.DMA((n // LANES,)),
        ],
        outs=[HB] + [VM] * 10,
    )
    arrived = lax.all_to_all(
        wire.reshape(n // 2, 2, LANES), "wide", split_axis=0, concat_axis=0,
        axis_index_groups=wide, tiled=True,
    ).reshape(n, LANES)
    halo_far = lax.ppermute(other, "narrow", other_pairs)
    halo_near = lax.ppermute(face, "narrow", pairs)

    full = own + 2 * SUB
    padded = full + 2 * PAD
    slots, take, take_rank, left, here, cloud, widened = call(
        route_kernel,
        [((peers, CAP * LANES), BF16), ((n, 2 * LANES), BF16), ((8, LANES), jnp.int32)]
        + [((levels, LANES), F32)] * 3
        + [((2, levels, padded, LANES), F32)],
        [VM] * 4, targets, crm, courant, cloud_mask,
    )
    started, _ = call(
        start_kernel, [((2, levels, full, LANES), F32), ((2, levels, padded, LANES), F32)],
        [VM] * 5, halo_near, halo_far, left, here, widened,
        room=6, alias={4: 1},
    )
    crm_new, diff = call(
        main_kernel,
        [((2, levels, own, LANES), BF16), ((2, ring * 4, LANES), F32)],
        [VM] * 9,
        arrived, take, take_rank, started, crm, left, here, cloud, down,
        scratch=[
            pltpu.VMEM((SUB, 2, ring * 4, LANES), F32),
            pltpu.VMEM((2, levels, padded, LANES), F32),
            pltpu.VMEM((2, levels, padded, LANES), F32),
            pltpu.VMEM((2, levels, own, LANES), BF16),
            pltpu.SemaphoreType.DMA((2 * PIECES,)),
        ],
        room=12,
        outs=[HB, VM],
    )
    rows = 2 * ring * 4 // NEAR
    parts = lax.all_to_all(
        diff.reshape(NEAR, rows, LANES), "narrow", split_axis=0, concat_axis=0,
        axis_index_groups=near, tiled=True,
    )
    sums = call(sum_kernel, [((NEAR, rows, LANES), F32)], [VM], parts)
    sums = lax.all_to_all(
        sums, "narrow", split_axis=0, concat_axis=0, axis_index_groups=far, tiled=True
    )
    back = call(turn_kernel, [((peers, LANES), F32)], [VM] * 2, sums, slots)
    back = lax.all_to_all(
        back.reshape(peers, 1, LANES), "wide", split_axis=0, concat_axis=0,
        axis_index_groups=wide, tiled=True,
    ).reshape(peers, LANES)
    change = call(back_kernel, [((NEAR, rows, LANES), F32)], [VM] * 3, back, owner, send_rank)
    change = lax.all_to_all(
        change, "narrow", split_axis=0, concat_axis=0, axis_index_groups=near, tiled=True
    )
    tendency = call(
        end_kernel, [((width, LANES), BF16)], [VM] * 2, change.reshape(NEAR * rows, LANES), up,
        scratch=[pltpu.VMEM((2, width // 2, LANES), BF16), pltpu.SemaphoreType.DMA((2,))],
        outs=HB,
    )
    return tendency.T, crm_new


def solution(mesh):
    placed = (
        P("wide", None),
        P(None, None, "narrow", "wide"),
        P(None, "wide"),
        P(None, "wide"),
        P(),
        P(),
        P(),
    )

    return jax.shard_map(
        shards,
        mesh=mesh,
        in_specs=placed,
        out_specs=(P("wide", None), P(None, None, "narrow", "wide")),
        check_vma=False,
    )
```

```python
import jax
import jax.numpy as jnp
from jax import lax
from jax.experimental import pallas as pl
from jax.experimental.pallas import tpu as pltpu
from jax.sharding import PartitionSpec as P


CX = 256
SUB = 4
CAP = 4
ROWS = 6
LANES = 128
EXTRA = 16
NEAR = 4
HEAD = 36
SIDE = 0.15
STEP = 1.0 / (0.1 * SIDE)
PAD = 8
PIECES = 3
UNROLL = 10
HI = lax.Precision.HIGHEST
F32 = jnp.float32
BF16 = jnp.bfloat16


def iota(shape, dim):
    return lax.broadcasted_iota(jnp.int32, shape, dim)


def dot(a, b, dims):
    return lax.dot_general(a, b, (dims, ((), ())), preferred_element_type=F32)


def split3(x):
    a = x.astype(BF16)
    r = x - a.astype(F32)
    b = r.astype(BF16)
    c = (r - b.astype(F32)).astype(BF16)
    return a, b, c


def row_parts(start):
    row = iota((LANES, LANES), 0) + start
    peer = (row * 10923) >> 16
    return peer ^ HEAD, row - peer * ROWS


def before_matrix():
    return (iota((LANES, LANES), 0) < iota((LANES, LANES), 1)).astype(BF16)


def pack_kernel(
    map_hbm, state_hbm, crm_hbm, courant_hbm, mask_hbm, down_hbm, up_hbm,
    wire_hbm, owner_ref, rank_ref, face_ref, other_ref,
    map_ref, crm_ref, courant_ref, mask_ref, down_ref, up_ref,
    state_ref, wire_ref, sems, out_sems,
):
    pairs = (
        (map_hbm, map_ref), (state_hbm, state_ref), (crm_hbm, crm_ref), (courant_hbm, courant_ref),
        (mask_hbm, mask_ref), (down_hbm, down_ref), (up_hbm, up_ref),
    )
    copies = [pltpu.make_async_copy(a, b, sems.at[i]) for i, (a, b) in enumerate(pairs)]
    for copy in copies:
        copy.start()
    copies[0].wait()
    peers = map_ref.shape[0]
    mine = map_ref[pl.ds(lax.axis_index("wide"), 1), :] >> 7
    own = (iota((peers, LANES), 0) ^ HEAD) == mine
    own_b = own.astype(BF16)
    count = dot(own_b, before_matrix(), ((1,), (0,)))
    rank = jnp.sum(jnp.where(own, count, 0.0), axis=0, keepdims=True).astype(jnp.int32)
    owner_ref[...] = own_b
    rank_ref[...] = jnp.broadcast_to(rank, rank_ref.shape)
    copies[1].wait()
    state = state_ref[...].astype(BF16)
    levels = state.shape[0]
    extra = state[LANES:levels].astype(F32)
    spread = [jnp.where(rank == k, extra, 0.0) for k in range(CAP)]
    spread.append(jnp.zeros((LANES - CAP * EXTRA, LANES), F32))
    spread = jnp.concatenate(spread, axis=0).astype(BF16)
    for start in range(0, peers * ROWS, LANES):
        peer, part = row_parts(start)
        to_peer = peer == mine
        main = (to_peer & (part == rank)).astype(BF16)
        tail = (to_peer & (part == CAP)).astype(BF16)
        wire = dot(main, state[:LANES], ((1,), (1,))) + dot(tail, spread, ((1,), (1,)))
        rows = pl.ds(start, LANES)
        wire_ref[rows] = wire.astype(BF16)
        out = pltpu.make_async_copy(
            wire_ref.at[rows], wire_hbm.at[rows], out_sems.at[start // LANES]
        )
        out.start()
        copies.append(out)
    copies[2].wait()
    own_columns = crm_ref.shape[2]
    odd = (lax.axis_index("narrow") & 1) == 1

    def faces(to_low, to_high):
        def body(level, carry):
            for f in range(2):
                to_low[f, level] = crm_ref[f, level, :SUB]
                to_high[f, level] = crm_ref[f, level, own_columns - SUB :]
            return carry

        lax.fori_loop(0, crm_ref.shape[1], body, 0, unroll=UNROLL)

    @pl.when(odd)
    def _():
        faces(face_ref, other_ref)

    @pl.when(jnp.logical_not(odd))
    def _():
        faces(other_ref, face_ref)

    for copy in copies[3:]:
        copy.wait()


def route_kernel(
    map_ref, crm_ref, courant_ref, mask_ref,
    slot_ref, take_ref, rank_ref, left_ref, here_ref, cloud_ref, wide_ref,
):
    own = crm_ref.shape[2]

    def widen(level, carry):
        q = crm_ref[1, level].astype(F32)
        m = crm_ref[0, level].astype(F32) + 2.0 * q
        for f, x in enumerate((m, q)):
            wide_ref[f, level, PAD : PAD + own] = x
            wide_ref[f, level, PAD + own + 2 * SUB : PAD + own + 2 * SUB + 1] = x[:1]
        return carry

    lax.fori_loop(0, crm_ref.shape[1], widen, 0, unroll=UNROLL)
    left_ref[...] = courant_ref[...] * (1.0 / SIDE) + 1.0
    here_ref[...] = (0.7 - courant_ref[...]) * (1.0 / SIDE)
    cloud_ref[...] = mask_ref[...].astype(F32) * 0.3
    peers = map_ref.shape[0]
    targets = map_ref[...]
    here = (targets >> 7) == lax.axis_index("wide")
    local = (targets & (LANES - 1)).astype(F32) + 1.0
    count = dot(here.astype(BF16), before_matrix(), ((1,), (0,)))
    slots = []
    lane = iota((peers, LANES), 1).astype(F32) + 1.0
    for k in range(CAP):
        hit = here & (count == float(k))
        one = jnp.sum(jnp.where(hit, local, 0.0), axis=1, keepdims=True)
        slots.append((one == lane).astype(F32))
    swap = ((iota((peers, peers), 0) ^ HEAD) == iota((peers, peers), 1)).astype(BF16)
    rank = jnp.zeros((1, LANES), F32)
    anyslot = jnp.zeros((peers, LANES), F32)
    for k in range(CAP):
        rank = rank + float(k) * jnp.sum(slots[k], axis=0, keepdims=True)
        anyslot = anyslot + slots[k]
        moved = dot(swap, slots[k].astype(BF16), ((1,), (0,)))
        slot_ref[:, k * LANES : (k + 1) * LANES] = moved.astype(BF16)
    rank_ref[...] = jnp.broadcast_to(rank, rank_ref.shape).astype(jnp.int32)
    n = peers * ROWS
    row = iota((n, peers), 0)
    peer = (row * 10923) >> 16
    part = row - peer * ROWS
    same = (peer ^ HEAD) == iota((n, peers), 1)
    main = jnp.zeros((n, LANES), F32)
    for k in range(CAP):
        main = main + dot((same & (part == k)).astype(BF16), slots[k].astype(BF16), ((1,), (0,)))
    tail = dot((same & (part == CAP)).astype(BF16), anyslot.astype(BF16), ((1,), (0,)))
    take_ref[:, :LANES] = main.astype(BF16)
    take_ref[:, LANES:] = tail.astype(BF16)


def mix(ref, f, level, left, here, rows):
    return (
        left * ref[f, level, PAD - 1 : PAD - 1 + rows]
        + here * ref[f, level, PAD : PAD + rows]
        + ref[f, level, PAD + 1 : PAD + 1 + rows]
    )


def put(ref, f, level, x):
    n = x.shape[0]
    ref[f, level, PAD : PAD + n] = x
    ref[f, level, PAD - 1 : PAD] = x[n - 1 :]
    ref[f, level, PAD + n : PAD + n + 1] = x[:1]


def column(levels, mixed, keep):
    def body(level, carry):
        below, here = carry
        above = mixed(jnp.minimum(level + 1, levels - 1))
        keep(level, [8.0 * h + (a + b) for a, h, b in zip(above, here, below, strict=True)])
        return here, above

    start = mixed(0)
    return body, (start, start)


def start_kernel(near_ref, far_ref, left_ref, here_ref, wide_ref, out_ref, load_ref):
    levels = near_ref.shape[1]
    rows = out_ref.shape[2]
    halo = 2 * SUB
    odd = (lax.axis_index("narrow") & 1) == 1

    def add_halo(high_ref, low_ref):
        def load(level, carry):
            sides = [
                jnp.concatenate([high_ref[f, level].astype(F32), low_ref[f, level].astype(F32)], axis=0)
                for f in range(2)
            ]
            sides[0] = sides[0] + 2.0 * sides[1]
            for f in range(2):
                load_ref[f, level, PAD + rows - halo : PAD + rows] = sides[f]
                load_ref[f, level, PAD - 1 : PAD] = sides[f][halo - 1 :]
            return carry

        lax.fori_loop(0, levels, load, 0, unroll=UNROLL)

    @pl.when(odd)
    def _():
        add_halo(far_ref, near_ref)

    @pl.when(jnp.logical_not(odd))
    def _():
        add_halo(near_ref, far_ref)

    def mixed(level):
        left, here = left_ref[pl.ds(level, 1), :], here_ref[pl.ds(level, 1), :]
        return tuple(mix(load_ref, f, level, left, here, rows) for f in range(2))

    def keep(level, pair):
        for f in range(2):
            out_ref[f, level] = pair[f]

    body, carry = column(levels, mixed, keep)
    lax.fori_loop(0, levels, body, carry, unroll=UNROLL)


def main_kernel(
    wire_ref, take_ref, rank_ref, start_ref, crm_ref, left_ref, here_ref, cloud_ref, down_ref,
    new_hbm, diff_ref, force_ref, field_ref, next_ref, new_ref, sems,
):
    levels = crm_ref.shape[1]
    gcm = down_ref.shape[1]
    own = crm_ref.shape[2]
    full = start_ref.shape[2]
    got = dot(wire_ref[...], take_ref[...], ((0,), (0,)))
    tail = jnp.zeros((EXTRA, LANES), F32)
    rank = rank_ref[0:1, :]
    for k in range(CAP):
        tail = tail + jnp.where(rank == k, got[k * EXTRA : (k + 1) * EXTRA, LANES:], 0.0)
    rows = jnp.concatenate([got[:, :LANES], tail], axis=0)
    force = [
        lax.dot_general(
            down_ref[...], rows[f * gcm : (f + 1) * gcm], (((1,), (0,)), ((), ())),
            precision=HI, preferred_element_type=F32,
        )
        for f in range(2)
    ]
    force[0] = force[0] + 2.0 * force[1]
    for index in range(SUB):
        for f in range(2):
            force_ref[index, f, :levels] = (0.25 * STEP ** (index + 1)) * force[f]
    diff_ref[...] = jnp.zeros_like(diff_ref)
    half = diff_ref.shape[0] // 2
    flip = jnp.where(lax.axis_index("narrow") < NEAR, diff_ref.shape[0] * 3 // NEAR, 0)

    def physics(pair, level, index):
        m = pair[0] + force_ref[index, 0, pl.ds(level, 1), :]
        q = pair[1] + force_ref[index, 1, pl.ds(level, 1), :]
        return m, q - cloud_ref[pl.ds(level, 1), :] * jnp.maximum(q, 0.0)

    def first(level, carry):
        pair = physics((start_ref[0, level], start_ref[1, level]), level, 0)
        for f in range(2):
            put(field_ref, f, level, pair[f])
        return carry

    lax.fori_loop(0, levels, first, 0, unroll=UNROLL)
    piece = levels // PIECES
    copies = []
    for index in range(1, SUB):
        last = index == SUB - 1
        source, target = (field_ref, next_ref) if index % 2 else (next_ref, field_ref)
        size = own if last else full

        def mixed(level, source=source, size=size):
            left, here = left_ref[pl.ds(level, 1), :], here_ref[pl.ds(level, 1), :]
            return tuple(mix(source, f, level, left, here, size) for f in range(2))

        def keep(level, pair, index=index, last=last, target=target):
            pair = physics(pair, level, index)
            if not last:
                for f in range(2):
                    put(target, f, level, pair[f])
                return
            scale = STEP**-SUB
            q = scale * pair[1]
            t = scale * pair[0] - 2.0 * q
            for f, x in enumerate((t, q)):
                new_ref[f, level] = x.astype(BF16)
                change = x - crm_ref[f, level].astype(F32)
                row = (f * half + level) ^ flip
                diff_ref[pl.ds(row, 1), :] = jnp.sum(change, axis=0, keepdims=True)

        body, carry = column(levels, mixed, keep)
        if not last:
            lax.fori_loop(0, levels, body, carry, unroll=UNROLL)
            continue
        for part in range(PIECES):
            carry = lax.fori_loop(part * piece, (part + 1) * piece, body, carry, unroll=UNROLL)
            span = pl.ds(part * piece, piece)
            for f in range(2):
                copy = pltpu.make_async_copy(
                    new_ref.at[f, span], new_hbm.at[f, span], sems.at[2 * part + f]
                )
                copy.start()
                copies.append(copy)
    for copy in copies:
        copy.wait()


def turn_kernel(part_ref, slot_ref, wire_ref):
    total = jnp.sum(part_ref[...], axis=0)
    peers = wire_ref.shape[0]
    rows = total.shape[0]
    wire = jnp.zeros((peers, LANES), F32)
    for piece in split3(total):
        for k in range(CAP):
            padded = []
            if k:
                padded.append(jnp.zeros((k * rows, LANES), F32))
            padded.append(piece.astype(F32))
            if (k + 1) * rows < LANES:
                padded.append(jnp.zeros((LANES - (k + 1) * rows, LANES), F32))
            block = jnp.concatenate(padded, axis=0).astype(BF16)
            wire = wire + dot(slot_ref[:, k * LANES : (k + 1) * LANES], block, ((1,), (1,)))
    wire_ref[...] = wire


def back_kernel(wire_ref, owner_ref, rank_ref, out_ref):
    rows = out_ref.shape[1]
    got = jnp.zeros((LANES, LANES), F32)
    for piece in split3(wire_ref[...]):
        got = got + dot(piece, owner_ref[...], ((0,), (0,)))
    rank = rank_ref[0:1, :]
    change = jnp.zeros((rows, LANES), F32)
    for k in range(CAP):
        change = change + jnp.where(rank == k, got[k * rows : (k + 1) * rows], 0.0)
    out_ref[...] = jnp.broadcast_to(change[None], out_ref.shape)


def sum_kernel(part_ref, out_ref):
    out_ref[...] = jnp.broadcast_to(jnp.sum(part_ref[...], axis=0)[None], out_ref.shape)


def end_kernel(change_ref, up_ref, out_hbm, out_ref, sems):
    levels, gcm = up_ref.shape
    half = change_ref.shape[0] // 2
    copies = []
    for f in range(2):
        tend = lax.dot_general(
            up_ref[...], change_ref[f * half : f * half + levels], (((0,), (0,)), ((), ())),
            precision=HI, preferred_element_type=F32,
        ) * (1.0 / (CX * SUB))
        rows = pl.ds(f * gcm, gcm)
        out_ref[f] = tend.astype(BF16)
        copy = pltpu.make_async_copy(out_ref.at[f], out_hbm.at[rows], sems.at[f])
        copy.start()
        copies.append(copy)
    for copy in copies:
        copy.wait()


VM = pl.BlockSpec(memory_space=pltpu.VMEM)
HB = pl.BlockSpec(memory_space=pltpu.HBM)


def call(kernel, shapes, specs, *args, scratch=(), room=4, outs=None, alias=None):
    out = [jax.ShapeDtypeStruct(s, d) for s, d in shapes]
    many = len(out) > 1
    return pl.pallas_call(
        kernel,
        out_shape=out if many else out[0],
        in_specs=specs,
        out_specs=outs or ([VM] * len(out) if many else VM),
        scratch_shapes=list(scratch),
        input_output_aliases=alias or {},
        compiler_params=pltpu.CompilerParams(vmem_limit_bytes=room << 20),
    )(*args)


def shards(gcm_state, crm_state, courant, cloud_mask, level_down, level_up, column_map):
    peers = lax.axis_size("wide")
    ring = lax.axis_size("narrow")
    columns, width = gcm_state.shape
    levels = crm_state.shape[1]
    own = crm_state.shape[2]
    targets = column_map.reshape(peers, columns)
    n = peers * ROWS
    wide = [[p ^ HEAD for p in range(peers)]]
    near = [[g * NEAR + i for i in reversed(range(NEAR))] for g in range(ring // NEAR)]
    far = [[g + NEAR * i for i in (2, 3, 1, 0)] for g in range(NEAR)]
    pairs = [(i, i ^ 1) for i in range(ring)]
    other_pairs = [(i, ((i + 1) ^ 1) - 1) for i in range(ring)]
    other_pairs = [(a, b % ring) for a, b in other_pairs]
    args = (targets, gcm_state.T, crm_state, courant, cloud_mask, level_down, level_up.T)
    resident = [(x.shape, x.dtype) for x in args]

    wire, owner, send_rank, face, other, targets, crm, courant, cloud_mask, down, up = call(
        pack_kernel,
        [((n, LANES), BF16), ((peers, LANES), BF16), ((8, LANES), jnp.int32)]
        + [((2, levels, SUB, LANES), BF16)] * 2
        + resident[:1] + resident[2:],
        [HB] * 7, *[pltpu.with_memory_space_constraint(x, pltpu.HBM) for x in args],
        scratch=[
            pltpu.VMEM((width, LANES), F32),
            pltpu.VMEM((n, LANES), BF16),
            pltpu.SemaphoreType.DMA((7,)),
            pltpu.SemaphoreType.DMA((n // LANES,)),
        ],
        outs=[HB] + [VM] * 10,
    )
    arrived = lax.all_to_all(
        wire.reshape(n // 2, 2, LANES), "wide", split_axis=0, concat_axis=0,
        axis_index_groups=wide, tiled=True,
    ).reshape(n, LANES)
    halo_far = lax.ppermute(other, "narrow", other_pairs)
    halo_near = lax.ppermute(face, "narrow", pairs)

    full = own + 2 * SUB
    padded = full + 2 * PAD
    slots, take, take_rank, left, here, cloud, widened = call(
        route_kernel,
        [((peers, CAP * LANES), BF16), ((n, 2 * LANES), BF16), ((8, LANES), jnp.int32)]
        + [((levels, LANES), F32)] * 3
        + [((2, levels, padded, LANES), F32)],
        [VM] * 4, targets, crm, courant, cloud_mask,
    )
    started, _ = call(
        start_kernel, [((2, levels, full, LANES), F32), ((2, levels, padded, LANES), F32)],
        [VM] * 5, halo_near, halo_far, left, here, widened,
        room=6, alias={4: 1},
    )
    crm_new, diff = call(
        main_kernel,
        [((2, levels, own, LANES), BF16), ((2 * ring * 4, LANES), F32)],
        [VM] * 9,
        arrived, take, take_rank, started, crm, left, here, cloud, down,
        scratch=[
            pltpu.VMEM((SUB, 2, ring * 4, LANES), F32),
            pltpu.VMEM((2, levels, padded, LANES), F32),
            pltpu.VMEM((2, levels, padded, LANES), F32),
            pltpu.VMEM((2, levels, own, LANES), BF16),
            pltpu.SemaphoreType.DMA((2 * PIECES,)),
        ],
        room=12,
        outs=[HB, VM],
    )
    rows = 2 * ring * 4 // NEAR
    parts = lax.all_to_all(
        diff.reshape(NEAR, rows, LANES), "narrow", split_axis=0, concat_axis=0,
        axis_index_groups=[near[0][::-1], *near[1:]], tiled=True,
    )
    sums = call(sum_kernel, [((NEAR, rows, LANES), F32)], [VM], parts)
    sums = lax.all_to_all(
        sums, "narrow", split_axis=0, concat_axis=0, axis_index_groups=far, tiled=True
    )
    back = call(turn_kernel, [((peers, LANES), F32)], [VM] * 2, sums, slots)
    back = lax.all_to_all(
        back.reshape(peers, 1, LANES), "wide", split_axis=0, concat_axis=0,
        axis_index_groups=wide, tiled=True,
    ).reshape(peers, LANES)
    change = call(back_kernel, [((NEAR, rows, LANES), F32)], [VM] * 3, back, owner, send_rank)
    change = lax.all_to_all(
        change, "narrow", split_axis=0, concat_axis=0, axis_index_groups=near, tiled=True
    )
    tendency = call(
        end_kernel, [((width, LANES), BF16)], [VM] * 2, change.reshape(NEAR * rows, LANES), up,
        scratch=[pltpu.VMEM((2, width // 2, LANES), BF16), pltpu.SemaphoreType.DMA((2,))],
        outs=HB,
    )
    return tendency.T, crm_new


def solution(mesh):
    placed = (
        P("wide", None),
        P(None, None, "narrow", "wide"),
        P(None, "wide"),
        P(None, "wide"),
        P(),
        P(),
        P(),
    )

    return jax.shard_map(
        shards,
        mesh=mesh,
        in_specs=placed,
        out_specs=(P("wide", None), P(None, None, "narrow", "wide")),
        check_vma=False,
    )
```
